32 devices in a mesh: row: 4 (over z), col: 8 (over y, x, core).
Axes of the slice: x: 2, y: 2, z: 4, core: 2. Of those that a mesh axis runs over, the one named last changes fastest.
Arguments:
- solution: float32 [8, 8, 4, 8, 256], P(None, None, 'row', 'col'), may hold values from -6 to 6
- residual: float32 [8, 8, 4, 8, 256], P(None, None, 'row', 'col'), may hold values from -120 to 120
- direction: float32 [8, 8, 4, 8, 256], P(None, None, 'row', 'col'), may hold values from -120 to 120
- noise_var: float32 [8, 4, 8, 256], P(None, 'row', 'col'), may hold values from 2 to 4
- coords: float32 [3, 8, 4, 8, 256], P(None, None, 'row', 'col'), may hold values from 0 to 128
- tile_pairs: int32 [2, 4, 8, 64], P(None, 'row', 'col'), may hold values from 0 to 63, as said below
- tile_count: int32 [4, 8], P('row', 'col'), may hold values from 1 to 64, as said below
Outputs:
- new_solution: float32 [8, 8, 4, 8, 256], P(None, None, 'row', 'col')
- new_residual: float32 [8, 8, 4, 8, 256], P(None, None, 'row', 'col')
- new_direction: float32 [8, 8, 4, 8, 256], P(None, None, 'row', 'col')
The draws below stay inside these ranges and needn't reach their ends.
Inputs may be any that keep to these rules, and one draw needn't show every extreme that they name: `tile_pairs`: entry [0, g, h, s] is one of the 64 row tiles of cell (g, h) and entry [1, g, h, s] one of its 32 column tiles; the first tile_count[g, h] pairs of a cell are distinct, and the mirror pair of each of them is live in the cell that holds it, so the kernel that the lists define is symmetric. `tile_count`: some cell holds exactly 64 live pairs.
All inputs are finite; a program needn't handle non-finite values.
Results may differ from the reference program's by a relative error of at most 0.0003.
Values sent between devices are 32-bit elements; how exact they have to be, the bound alone decides.
No kernel may reach another device: no remote copies, remote signals or barrier semaphores. Data moves between devices by JAX's collectives and lax.ppermute only.
A program may use at most 64 MiB of HBM per device.

```python
import math
import jax
import jax.numpy as jnp
from jax import lax

TILE = 256
RHS = 8
TPD = 8
GRID_ROWS = 4
GRID_COLS = 8
TILES = 256
NNZ = 64


def spread_bits(index_value, offset):
    result = jnp.zeros_like(index_value)
    for bit_level in range(8):
        result = result + index_value // 2 ** (3 * bit_level + offset) % 2 * 2 ** bit_level
    return result


def lattice(key):
    block_count = TPD * GRID_ROWS
    block_index = jnp.arange(block_count, dtype=jnp.int32)
    block_x = spread_bits(block_index, 2)
    block_y = spread_bits(block_index, 1)
    block_z = spread_bits(block_index, 0)
    heavy_row = jax.random.randint(jax.random.fold_in(key, 7001), (), 0, GRID_ROWS)
    is_heavy = block_index % GRID_ROWS == heavy_row
    block_keys = jax.random.split(jax.random.fold_in(key, 7002), block_count)
    orders = jax.vmap(lambda block_key: jax.random.permutation(block_key, 64))(block_keys)
    light_codes = jnp.sort(orders[:, :GRID_COLS].astype(jnp.int32), axis=1)
    light_x = light_codes // 4 % 2 + 2 * (light_codes // 32 % 2)
    light_y = light_codes // 2 % 2 + 2 * (light_codes // 16 % 2)
    light_z = light_codes % 2 + 2 * (light_codes // 8 % 2)
    slot_index = jnp.arange(GRID_COLS, dtype=jnp.int32)
    corner = slot_index // (GRID_COLS // 8)
    heavy_x = jnp.broadcast_to((1 + corner // 4 % 2)[None, :], light_codes.shape)
    heavy_y = jnp.broadcast_to((1 + corner // 2 % 2)[None, :], light_codes.shape)
    heavy_z = jnp.broadcast_to((1 + corner % 2)[None, :], light_codes.shape)
    local_x = jnp.where(is_heavy[:, None], heavy_x, light_x)
    local_y = jnp.where(is_heavy[:, None], heavy_y, light_y)
    local_z = jnp.where(is_heavy[:, None], heavy_z, light_z)
    cell_x = (4 * block_x[:, None] + local_x).reshape(-1).astype(jnp.int32)
    cell_y = (4 * block_y[:, None] + local_y).reshape(-1).astype(jnp.int32)
    cell_z = (4 * block_z[:, None] + local_z).reshape(-1).astype(jnp.int32)
    return (cell_x, cell_y, cell_z)


def pair_lists(key):
    cell_x, cell_y, cell_z = lattice(key)
    row_tiles = GRID_COLS * TPD
    col_tiles = GRID_ROWS * TPD
    grid_size = row_tiles * col_tiles
    devices = GRID_ROWS * GRID_COLS
    full_shape = (GRID_ROWS, GRID_COLS, row_tiles, col_tiles)
    local_row = jnp.arange(row_tiles, dtype=jnp.int32)
    local_col = jnp.arange(col_tiles, dtype=jnp.int32)
    row_index = jnp.arange(GRID_ROWS, dtype=jnp.int32)
    col_index = jnp.arange(GRID_COLS, dtype=jnp.int32)
    row_tile = (local_row[None, :] // GRID_COLS * GRID_ROWS + row_index[:, None]) * GRID_COLS + local_row[None, :] % GRID_COLS
    col_tile = (local_col[None, :] // GRID_ROWS * GRID_ROWS + local_col[None, :] % GRID_ROWS) * GRID_COLS + col_index[:, None]
    row_grid = jnp.broadcast_to(row_tile[:, None, :, None], full_shape)
    col_grid = jnp.broadcast_to(col_tile[None, :, None, :], full_shape)
    adjacent = (jnp.abs(cell_x[row_grid] - cell_x[col_grid]) <= 1) & (jnp.abs(cell_y[row_grid] - cell_y[col_grid]) <= 1) & (jnp.abs(cell_z[row_grid] - cell_z[col_grid]) <= 1)
    self_pair = row_grid == col_grid
    device_keys = jax.random.split(jax.random.fold_in(key, 7003), devices)
    ranks = jax.vmap(lambda dev_key: jax.random.permutation(dev_key, grid_size))(device_keys)
    ranks = ranks.astype(jnp.int32).reshape(full_shape)
    first_score = jnp.where(self_pair, ranks - grid_size, jnp.where(adjacent, ranks, grid_size + ranks))
    position = jnp.argsort(jnp.argsort(first_score.reshape(devices, grid_size), axis=1), axis=1).reshape(full_shape)
    kept_pairs = adjacent & (position < NNZ)
    pair_table = jnp.zeros((TILES, TILES), jnp.int32).at[row_grid.ravel(), col_grid.ravel()].set(kept_pairs.ravel().astype(jnp.int32))
    mirrored = pair_table * pair_table.T
    final_pairs = mirrored[row_grid, col_grid] > 0
    second_score = jnp.where(final_pairs, ranks, grid_size + ranks)
    picked = jnp.argsort(second_score.reshape(devices, grid_size), axis=1)[:, :NNZ].astype(jnp.int32)
    pair_array = jnp.stack([picked // col_tiles, picked % col_tiles]).reshape(2, GRID_ROWS, GRID_COLS, NNZ)
    live_count = jnp.sum(final_pairs.astype(jnp.int32), axis=(2, 3))
    return (pair_array.astype(jnp.int32), live_count.astype(jnp.int32))


def draw_tile_pairs(key, part):
    pair_array, counts = pair_lists(key)
    return pair_array


def draw_tile_count(key, part):
    pair_array, counts = pair_lists(key)
    return counts


def draw_coords(key, part):
    cell_x, cell_y, cell_z = lattice(key)
    sub_index = jnp.arange(TILE, dtype=jnp.int32)
    sub_x = (sub_index % 4).astype(jnp.float32)
    sub_y = (sub_index // 4 % 4).astype(jnp.float32)
    sub_z = (sub_index // 16).astype(jnp.float32)
    layers = TILE // 16
    jitter = jax.random.uniform(jax.random.fold_in(key, 7005), (3, TILES, TILE))
    coord_x = cell_x[:, None].astype(jnp.float32) + (sub_x[None, :] + jitter[0]) / 4.0
    coord_y = cell_y[:, None].astype(jnp.float32) + (sub_y[None, :] + jitter[1]) / 4.0
    coord_z = cell_z[:, None].astype(jnp.float32) + (sub_z[None, :] + jitter[2]) / layers
    stacked = jnp.stack([coord_x, coord_y, coord_z])
    return stacked.reshape(3, TPD, GRID_ROWS, GRID_COLS, TILE).astype(jnp.float32)


def scaled_field(key, salt_base):
    field_shape = (RHS, TPD, GRID_ROWS, GRID_COLS, TILE)
    base_field = jax.random.normal(jax.random.fold_in(key, salt_base), field_shape)
    base_field = jnp.clip(base_field, -4.0, 4.0)
    point_scale = jnp.exp(math.log(10.0) * (jax.random.uniform(jax.random.fold_in(key, salt_base + 3), field_shape[1:]) - 0.5))
    side_scale = jnp.exp(math.log(10.0) * (jax.random.uniform(jax.random.fold_in(key, salt_base + 4), (RHS,)) - 0.5))
    device_place = (jnp.arange(GRID_ROWS)[:, None] * GRID_COLS + jnp.arange(GRID_COLS)[None, :]) / (GRID_ROWS * GRID_COLS - 1)
    device_ramp = jnp.exp(math.log(3.0) * (device_place - 0.5))
    scaled = base_field * side_scale[:, None, None, None, None] * point_scale[None] * device_ramp[None, None, :, :, None]
    return scaled.astype(jnp.float32)


def draw_residual(key, part):
    return scaled_field(key, 7100)


def draw_direction(key, part):
    return scaled_field(key, 7200)


def block_scale(stream_key, dims, shards, smallest, high):
    loudness, own = 1.0, jax.random.fold_in(stream_key, 6)
    for dim, blocks in shards:
        draws = jnp.exp(jax.random.uniform(jax.random.fold_in(own, dim), (blocks,), jnp.float32, smallest / len(shards), high / len(shards)))
        loudness = loudness * jnp.repeat(draws, dims[dim] // blocks).reshape([-1 if axis == dim else 1 for axis in range(len(dims))])
    return loudness


def noise(key, dims, width, bound, pieces=(), held_as=jnp.bfloat16):
    factor_of = block_scale(key, dims, pieces, -0.22, 0.18) if pieces else 1.0
    values = jax.random.normal(key, dims, jnp.float32) * width * factor_of
    return jnp.minimum(jnp.maximum(values, -bound), bound).astype(held_as)


def setup_inputs(seed: int = 0) -> dict:
    arg_keys = jax.random.split(jax.random.key(seed), 8)
    solution = noise(arg_keys[0], (RHS, TPD, GRID_ROWS, GRID_COLS, TILE), 1.0, 6.0, ((2, 4), (3, 8)), jnp.float32)
    residual = draw_residual(jax.random.fold_in(arg_keys[7], 71), 0)
    direction = draw_direction(jax.random.fold_in(arg_keys[7], 71), 0)
    noise_var = jnp.clip(jnp.exp(math.log(4.0) - 0.6931472 * jax.random.uniform(arg_keys[3], (TPD, GRID_ROWS, GRID_COLS, TILE), jnp.float32) ** block_scale(arg_keys[3], (TPD, GRID_ROWS, GRID_COLS, TILE), ((1, 4), (2, 8)), -0.2, 0.2)), 2.0, 4.0)
    coords = draw_coords(jax.random.fold_in(arg_keys[7], 71), 0)
    tile_pairs = draw_tile_pairs(jax.random.fold_in(arg_keys[7], 71), 0)
    tile_count = draw_tile_count(jax.random.fold_in(arg_keys[7], 71), 0)
    return {"solution": solution, "residual": residual, "direction": direction, "noise_var": noise_var, "coords": coords, "tile_pairs": tile_pairs, "tile_count": tile_count}


EPS = 1e-06
KERNEL_SCALE = 0.125
HIGHEST = lax.Precision.HIGHEST

def wendland(target_pts, source_pts):
    delta_x = target_pts[0][:, None] - source_pts[0][None, :]
    delta_y = target_pts[1][:, None] - source_pts[1][None, :]
    delta_z = target_pts[2][:, None] - source_pts[2][None, :]
    distance = jnp.sqrt(delta_x * delta_x + delta_y * delta_y + delta_z * delta_z)
    reach_left = jnp.maximum(1.0 - distance, 0.0)
    squared = reach_left * reach_left
    return squared * squared * (4.0 * distance + 1.0)

def kernel_product(direction, coords, tile_pairs, tile_count):
    tiles_all = TPD * GRID_ROWS * GRID_COLS
    points = coords.reshape(3, tiles_all, TILE)
    values = direction.reshape(RHS, tiles_all, TILE)
    pair_rows = tile_pairs[0].reshape(GRID_ROWS * GRID_COLS, NNZ)
    pair_cols = tile_pairs[1].reshape(GRID_ROWS * GRID_COLS, NNZ)
    counts = tile_count.reshape(GRID_ROWS * GRID_COLS)

    def one_cell(grid_cell, totals):
        grid_row = grid_cell // GRID_COLS
        grid_col = grid_cell % GRID_COLS

        def one_pair(pair_slot, inner_totals):
            row_local = pair_rows[grid_cell, pair_slot]
            col_local = pair_cols[grid_cell, pair_slot]
            row_tile = (row_local // GRID_COLS * GRID_ROWS + grid_row) * GRID_COLS + row_local % GRID_COLS
            col_tile = (col_local // GRID_ROWS * GRID_ROWS + col_local % GRID_ROWS) * GRID_COLS + grid_col
            kernel_block = wendland(lax.dynamic_index_in_dim(points, row_tile, 1, False), lax.dynamic_index_in_dim(points, col_tile, 1, False))
            source = lax.dynamic_index_in_dim(values, col_tile, 1, False)
            contrib = jnp.dot(source, kernel_block.T, precision=HIGHEST, preferred_element_type=jnp.float32)
            current = lax.dynamic_index_in_dim(inner_totals, row_tile, 1, True)
            return lax.dynamic_update_index_in_dim(inner_totals, current + contrib[:, None, :], row_tile, 1)
        return lax.fori_loop(jnp.int32(0), counts[grid_cell], one_pair, totals)
    zero_totals = jnp.zeros((RHS, tiles_all, TILE), jnp.float32)
    summed = lax.fori_loop(jnp.int32(0), jnp.int32(GRID_ROWS * GRID_COLS), one_cell, zero_totals)
    return summed.reshape(direction.shape)

def reference(solution, residual, direction, noise_var, coords, tile_pairs, tile_count):
    kernel_part = kernel_product(direction, coords, tile_pairs, tile_count)
    applied = noise_var[None] * direction + KERNEL_SCALE * kernel_part
    norm_now = lax.optimization_barrier(jnp.sum(residual * residual, axis=(1, 2, 3, 4)))
    curvature = lax.optimization_barrier(jnp.sum(direction * applied, axis=(1, 2, 3, 4)))
    step_size = (norm_now / curvature)[:, None, None, None, None]
    new_solution = solution + step_size * direction
    new_residual = residual - step_size * applied
    norm_next = lax.optimization_barrier(jnp.sum(new_residual * new_residual, axis=(1, 2, 3, 4)))
    beta_ratio = (norm_next / (norm_now + EPS))[:, None, None, None, None]
    new_direction = new_residual + beta_ratio * direction
    return (new_solution, new_residual, new_direction)
```

```python
import functools
import jax
import jax.numpy as jnp
from jax import lax
from jax.experimental import pallas as pl
from jax.experimental.pallas import tpu as pltpu
from jax.sharding import PartitionSpec as P

EPS = 1e-06
SCALED_KERNEL = 0.125 / 256.0
TINY = 1e-30
LANES = 128
SLAB = 256


def pair_kernel(rows, cols, owned, count_ref, pairs_ref, *refs):
    sources = refs[:cols]
    targets = refs[cols : cols + rows]
    outs = refs[cols + rows : cols + 2 * rows]
    slab, spots, totals = refs[cols + 2 * rows :]
    my_row = lax.axis_index("row")
    my_col = lax.axis_index("col")
    spread = sources[0].shape[0]
    for shift in range(cols):
        slab[lax.rem(my_col - shift + cols, cols), pl.ds(0, spread), :] = sources[shift][...]
    for shift in range(rows):
        spots[lax.rem(my_row - shift + rows, rows)] = 4.0 * targets[shift][...]
    totals[...] = jnp.zeros_like(totals)
    sides = 8
    stride = 2 * owned
    held = sides * stride

    def add_pair(slot, carry):
        row_tile = pairs_ref[0, slot]
        col_tile = pairs_ref[1, slot]
        origin = lax.rem(row_tile, cols)
        lane_row = 2 * lax.div(row_tile, cols)
        owner = lax.rem(col_tile, rows)
        spot_row = 2 * lax.div(col_tile, rows)
        spot = [
            [spots[owner, pl.ds(axis * stride + spot_row + half, 1), :] for axis in range(3)]
            for half in range(2)
        ]
        high_parts, low_parts, lhs_parts = [], [], []
        for side in range(2):
            values = slab[origin, pl.ds(lane_row + side, sides, stride=stride), :]
            lead = values.astype(jnp.bfloat16)
            rest = (values - lead.astype(jnp.float32)).astype(jnp.bfloat16)
            lhs_parts.append(jnp.concatenate([lead, rest], axis=0))
            points = 4.0 * slab[origin, pl.ds(held + lane_row + side, sides, stride=stride), :]
            turned = jnp.transpose(points)
            for step in range(LANES // 16):
                part = turned[16 * step : 16 * step + 16]
                grid = [jnp.broadcast_to(part[:, axis : axis + 1], (16, LANES)) for axis in range(3)]
                halves_high, halves_low = [], []
                for half in range(2):
                    dx = grid[0] - spot[half][0]
                    dy = grid[1] - spot[half][1]
                    dz = grid[2] - spot[half][2]
                    square = dx * dx + dy * dy + dz * dz
                    distance = square * lax.rsqrt(jnp.maximum(square, TINY))
                    left = jnp.maximum(4.0 - distance, 0.0)
                    left = left * left
                    weight = left * left * (distance + 1.0)
                    high = weight.astype(jnp.bfloat16)
                    halves_high.append(high)
                    halves_low.append((weight - high.astype(jnp.float32)).astype(jnp.bfloat16))
                high_parts.append(jnp.concatenate(halves_high, axis=1))
                low_parts.append(jnp.concatenate(halves_low, axis=1))
        lhs = jnp.concatenate(lhs_parts, axis=1)
        product = jnp.dot(
            lhs, jnp.concatenate(high_parts, axis=0), preferred_element_type=jnp.float32
        ) + jnp.dot(lhs, jnp.concatenate(low_parts, axis=0), preferred_element_type=jnp.float32)
        summed = product[:sides] + product[sides:]
        for half in range(2):
            totals[owner, spot_row + half] += summed[:, LANES * half : LANES * half + LANES]
        return carry

    lax.fori_loop(0, count_ref[0, 0], add_pair, jnp.int32(0))
    for shift in range(rows):
        outs[shift][...] = totals[lax.rem(my_row + shift, rows)]


def sums_kernel(rows, parts, residual_ref, direction_ref, noise_ref, *refs):
    partials = refs[:rows]
    applied_ref, stats_ref, stack = refs[rows:]
    halves = noise_ref.shape[0]
    sides = residual_ref.shape[0] // halves
    zero = jnp.zeros((sides, LANES), jnp.float32)
    now, bend, cross, size = zero, zero, zero, zero
    for part in range(halves):
        total = partials[0][part]
        for other in partials[1:]:
            total = total + other[part]
        residual = residual_ref[pl.ds(part, sides, stride=halves), :]
        direction = direction_ref[pl.ds(part, sides, stride=halves), :]
        applied = noise_ref[part : part + 1, :] * direction + SCALED_KERNEL * total
        applied_ref[part] = applied
        now = now + residual * residual
        bend = bend + direction * applied
        cross = cross + residual * applied
        size = size + applied * applied
    stack[...] = jnp.zeros_like(stack)
    for slot, value in enumerate((now, bend, cross, size)):
        stack[sides * slot : sides * slot + sides, :] = value
    stats_ref[...] = lax.dot_general(
        jnp.ones((parts, LANES), jnp.float32),
        stack[...],
        (((1,), (1,)), ((), ())),
        precision=lax.Precision.HIGHEST,
        preferred_element_type=jnp.float32,
    )


def step_kernel(
    stats_ref, applied_ref, solution_ref, residual_ref, direction_ref, new_x, new_r, new_d
):
    halves = applied_ref.shape[0]
    sides = applied_ref.shape[1]
    summed = jnp.sum(stats_ref[...], axis=0, keepdims=True)
    summed = jnp.broadcast_to(summed, (sides, LANES))
    lane = lax.broadcasted_iota(jnp.int32, (sides, LANES), 1)
    line = lax.broadcasted_iota(jnp.int32, (sides, LANES), 0)

    def pick(slot):
        return jnp.sum(
            jnp.where(lane == line + sides * slot, summed, 0.0), axis=1, keepdims=True
        )

    now, bend, cross, size = pick(0), pick(1), pick(2), pick(3)
    step = now / bend
    after = jnp.maximum(now - 2.0 * step * cross + step * step * size, 0.0)
    beta = jnp.broadcast_to(after / (now + EPS), (sides, LANES))
    step = jnp.broadcast_to(step, (sides, LANES))
    for part in range(halves):
        place = pl.ds(part, sides, stride=halves)
        direction = direction_ref[place, :]
        new_x[place, :] = solution_ref[place, :] + step * direction
        residual = residual_ref[place, :] - step * applied_ref[part]
        new_r[place, :] = residual
        new_d[place, :] = residual + beta * direction


def per_device(rows, cols, solution, residual, direction, noise_var, coords, tile_pairs, tile_count):
    sides, owned, _, _, tile_size = direction.shape
    parts = rows * cols
    halves = owned * tile_size // LANES
    flat_x = solution.reshape(-1, LANES)
    flat_r = residual.reshape(-1, LANES)
    flat_d = direction.reshape(-1, LANES)
    flat_c = coords.reshape(-1, LANES)
    mine = jnp.concatenate([flat_d, flat_c], axis=0)
    sources = [mine] + [
        lax.ppermute(mine, "col", [(at, (at + shift) % cols) for at in range(cols)])
        for shift in range(1, cols)
    ]
    targets = [flat_c] + [
        lax.ppermute(flat_c, "row", [(at, (at + shift) % rows) for at in range(rows)])
        for shift in range(1, rows)
    ]
    vmem = pl.BlockSpec(memory_space=pltpu.VMEM)
    smem = pl.BlockSpec(memory_space=pltpu.SMEM)
    block = jax.ShapeDtypeStruct((halves, sides, LANES), jnp.float32)
    flat = jax.ShapeDtypeStruct(flat_d.shape, jnp.float32)
    partials = pl.pallas_call(
        functools.partial(pair_kernel, rows, cols, owned),
        out_shape=[block] * rows,
        in_specs=[smem, smem] + [vmem] * (cols + rows),
        out_specs=[vmem] * rows,
        scratch_shapes=[
            pltpu.VMEM((cols, SLAB, LANES), jnp.float32),
            pltpu.VMEM((rows,) + flat_c.shape, jnp.float32),
            pltpu.VMEM((rows, halves, sides, LANES), jnp.float32),
        ],
        compiler_params=pltpu.CompilerParams(vmem_limit_bytes=32 << 20),
        name="pairs",
    )(tile_count, tile_pairs.reshape(2, -1), *sources, *targets)
    partials = [partials[0]] + [
        lax.ppermute(partials[shift], "row", [(at, (at + shift) % rows) for at in range(rows)])
        for shift in range(1, rows)
    ]
    applied, stats = pl.pallas_call(
        functools.partial(sums_kernel, rows, parts),
        out_shape=[block, jax.ShapeDtypeStruct((parts, LANES), jnp.float32)],
        in_specs=[vmem] * (3 + rows),
        out_specs=[vmem] * 2,
        scratch_shapes=[pltpu.VMEM((LANES, LANES), jnp.float32)],
        name="sums",
    )(flat_r, flat_d, noise_var.reshape(-1, LANES), *partials)
    stats = lax.all_to_all(stats, ("row", "col"), 0, 0, tiled=True)
    new_x, new_r, new_d = pl.pallas_call(
        step_kernel,
        out_shape=[flat] * 3,
        in_specs=[vmem] * 5,
        out_specs=[vmem] * 3,
        name="step",
    )(stats, applied, flat_x, flat_r, flat_d)
    return tuple(new.reshape(direction.shape) for new in (new_x, new_r, new_d))


def solution(mesh):
    field = P(None, None, "row", "col", None)
    in_specs = (field, field, field, P(None, "row", "col", None), field, P(None, "row", "col", None), P("row", "col"))
    return jax.shard_map(
        functools.partial(per_device, mesh.shape["row"], mesh.shape["col"]),
        mesh=mesh,
        in_specs=in_specs,
        out_specs=(field, field, field),
        check_vma=False,
    )
```

```python
import functools
import jax
import jax.numpy as jnp
from jax import lax
from jax.experimental import pallas as pl
from jax.experimental.pallas import tpu as pltpu
from jax.sharding import PartitionSpec as P

EPS = 1e-06
SCALED_KERNEL = 0.125 / 256.0
TINY = 1e-30
LANES = 128
SLAB = 256


def scratch(rows, cols, owned):
    return [
        pltpu.VMEM((cols, SLAB, LANES), jnp.float32),
        pltpu.VMEM((rows, owned, 3, 2 * LANES, LANES), jnp.float32),
        pltpu.VMEM((rows, 2 * owned, 8, LANES), jnp.float32),
        pltpu.SMEM((rows * owned,), jnp.int32),
    ]


def pair_kernel(rows, cols, owned, count_ref, pairs_ref, *refs):
    sources = refs[:2]
    targets = refs[2:4]
    outs = refs[4 : 4 + rows]
    slab, spots, totals, wanted = refs[4 + rows :]
    my_row = lax.axis_index("row")
    my_col = lax.axis_index("col")
    sides = 8
    stride = 2 * owned
    held = sides * stride
    spread = 3 * stride
    for place, mask in enumerate(masks(cols)):
        stack = sources[place // (cols // 2)]
        top = (place % (cols // 2)) * (held + spread)
        origin = lax.bitwise_xor(my_col, mask)
        slab[origin, pl.ds(0, held), :] = stack[pl.ds(top, held), :]
        slab[origin, pl.ds(held, spread), :] = 4.0 * stack[pl.ds(top + held, spread), :]
    for tile in range(rows * owned):
        wanted[tile] = 0
    for slot in range(pairs_ref.shape[1]):
        wanted[pairs_ref[1, slot]] = 1
    for place, mask in enumerate(masks(rows)):
        owner = lax.bitwise_xor(my_row, mask)
        top = (place % (rows // 2)) * spread
        turned = 4.0 * jnp.transpose(targets[place // (rows // 2)][pl.ds(top, spread), :])
        for tile in range(owned):

            @pl.when(wanted[tile * rows + owner] == 1)
            def _():
                for axis in range(3):
                    for half in range(2):
                        lane = axis * stride + 2 * tile + half
                        spots[owner, tile, axis, pl.ds(LANES * half, LANES), :] = jnp.broadcast_to(
                            turned[:, lane : lane + 1], (LANES, LANES)
                        )

    totals[...] = jnp.zeros_like(totals)

    def add_pair(slot, carry):
        row_tile = pairs_ref[0, slot]
        col_tile = pairs_ref[1, slot]
        origin = lax.rem(row_tile, cols)
        lane_row = 2 * lax.div(row_tile, cols)
        owner = lax.rem(col_tile, rows)
        spot_tile = lax.div(col_tile, rows)
        lhs_parts = []
        near = []
        for side in range(2):
            values = slab[origin, pl.ds(lane_row + side, sides, stride=stride), :]
            lead = values.astype(jnp.bfloat16)
            rest = (values - lead.astype(jnp.float32)).astype(jnp.bfloat16)
            lhs_parts.append(jnp.concatenate([lead, rest], axis=0))
            near.append(
                [
                    jnp.broadcast_to(slab[origin, pl.ds(held + axis * stride + lane_row + side, 1), :], (16, LANES))
                    for axis in range(3)
                ]
            )
        high_parts, low_parts = [], []
        for step in range(2 * LANES // 16):
            grid = [spots[owner, spot_tile, axis, pl.ds(16 * step, 16), :] for axis in range(3)]
            halves_high, halves_low = [], []
            for side in range(2):
                dx = grid[0] - near[side][0]
                dy = grid[1] - near[side][1]
                dz = grid[2] - near[side][2]
                square = dx * dx + dy * dy + dz * dz
                distance = square * lax.rsqrt(jnp.maximum(square, TINY))
                left = jnp.maximum(4.0 - distance, 0.0)
                left = left * left
                weight = left * left * (distance + 1.0)
                high = weight.astype(jnp.bfloat16)
                halves_high.append(high)
                halves_low.append((weight - high.astype(jnp.float32)).astype(jnp.bfloat16))
            high_parts.append(jnp.concatenate(halves_high, axis=1))
            low_parts.append(jnp.concatenate(halves_low, axis=1))
        lhs = jnp.concatenate(lhs_parts, axis=1)
        dims = (((1,), (1,)), ((), ()))
        product = lax.dot_general(
            lhs, jnp.concatenate(high_parts, axis=0), dims, preferred_element_type=jnp.float32
        ) + lax.dot_general(
            lhs, jnp.concatenate(low_parts, axis=0), dims, preferred_element_type=jnp.float32
        )
        summed = product[:sides] + product[sides:]
        for half in range(2):
            totals[owner, 2 * spot_tile + half] += summed[:, LANES * half : LANES * half + LANES]
        return carry

    count = count_ref[0, 0]
    whole = lax.div(count, 8)

    def add_group(step, carry):
        for part in range(8):
            add_pair(8 * step + part, carry)
        return carry

    lax.fori_loop(0, whole, add_group, jnp.int32(0))
    lax.fori_loop(8 * whole, count, add_pair, jnp.int32(0))
    for shift in range(rows):
        outs[shift][...] = totals[lax.rem(my_row + shift, rows)]


def sums_kernel(rows, parts, residual_ref, direction_ref, noise_ref, *refs):
    partials = refs[:rows]
    applied_ref, stats_ref, stack = refs[rows:]
    halves = noise_ref.shape[0]
    sides = residual_ref.shape[0] // halves
    zero = jnp.zeros((sides, LANES), jnp.float32)
    now, bend, cross, size = zero, zero, zero, zero
    for part in range(halves):
        total = partials[0][part]
        for other in partials[1:]:
            total = total + other[part]
        residual = residual_ref[pl.ds(part, sides, stride=halves), :]
        direction = direction_ref[pl.ds(part, sides, stride=halves), :]
        applied = noise_ref[part : part + 1, :] * direction + SCALED_KERNEL * total
        applied_ref[part] = applied
        now = now + residual * residual
        bend = bend + direction * applied
        cross = cross + residual * applied
        size = size + applied * applied
    stack[...] = jnp.zeros_like(stack)
    for slot, value in enumerate((now, bend, cross, size)):
        stack[sides * slot : sides * slot + sides, :] = value
    stats_ref[...] = lax.dot_general(
        jnp.ones((parts, LANES), jnp.float32),
        stack[...],
        (((1,), (1,)), ((), ())),
        precision=lax.Precision.HIGHEST,
        preferred_element_type=jnp.float32,
    )


def step_kernel(
    stats_ref, applied_ref, solution_ref, residual_ref, direction_ref, new_x, new_r, new_d
):
    halves = applied_ref.shape[0]
    sides = applied_ref.shape[1]
    summed = jnp.sum(stats_ref[...], axis=0, keepdims=True)
    summed = jnp.broadcast_to(summed, (sides, LANES))
    lane = lax.broadcasted_iota(jnp.int32, (sides, LANES), 1)
    line = lax.broadcasted_iota(jnp.int32, (sides, LANES), 0)

    def pick(slot):
        return jnp.sum(
            jnp.where(lane == line + sides * slot, summed, 0.0), axis=1, keepdims=True
        )

    now, bend, cross, size = pick(0), pick(1), pick(2), pick(3)
    step = now / bend
    after = jnp.maximum(now - 2.0 * step * cross + step * step * size, 0.0)
    beta = jnp.broadcast_to(after / (now + EPS), (sides, LANES))
    step = jnp.broadcast_to(step, (sides, LANES))
    for part in range(halves):
        place = pl.ds(part, sides, stride=halves)
        direction = direction_ref[place, :]
        new_x[place, :] = solution_ref[place, :] + step * direction
        residual = residual_ref[place, :] - step * applied_ref[part]
        new_r[place, :] = residual
        new_d[place, :] = residual + beta * direction


def doubled(blocks, axes, sizes):
    held = list(blocks)
    bits = [size // 2 for size in sizes]
    out = [None] * len(held)
    while any(bits):
        live = [at for at, bit in enumerate(bits) if bit]
        moved = {
            at: lax.ppermute(held[at], axes[at], [(to, to ^ bits[at]) for to in range(sizes[at])])
            for at in live
        }
        moved = dict(zip(live, lax.optimization_barrier(tuple(moved[at] for at in live))))
        for at in live:
            if bits[at] == 1:
                out[at] = [held[at], moved[at]]
            else:
                held[at] = jnp.concatenate([held[at], moved[at]], axis=0)
            bits[at] //= 2
    return out


def masks(size):
    found = [0]
    bit = size // 2
    while bit:
        found = found + [mask ^ bit for mask in found]
        bit //= 2
    return found


def per_device(rows, cols, solution, residual, direction, noise_var, coords, tile_pairs, tile_count):
    sides, owned, _, _, tile_size = direction.shape
    parts = rows * cols
    halves = owned * tile_size // LANES
    flat_x = solution.reshape(-1, LANES)
    flat_r = residual.reshape(-1, LANES)
    flat_d = direction.reshape(-1, LANES)
    flat_c = coords.reshape(-1, LANES)
    mine = jnp.concatenate([flat_d, flat_c], axis=0)
    sources, targets = doubled((mine, flat_c), ("col", "row"), (cols, rows))
    vmem = pl.BlockSpec(memory_space=pltpu.VMEM)
    smem = pl.BlockSpec(memory_space=pltpu.SMEM)
    block = jax.ShapeDtypeStruct((halves, sides, LANES), jnp.float32)
    flat = jax.ShapeDtypeStruct(flat_d.shape, jnp.float32)
    partials = pl.pallas_call(
        functools.partial(pair_kernel, rows, cols, owned),
        out_shape=[block] * rows,
        in_specs=[smem, smem] + [vmem] * 4,
        out_specs=[vmem] * rows,
        scratch_shapes=scratch(rows, cols, owned),
        compiler_params=pltpu.CompilerParams(vmem_limit_bytes=32 << 20),
        name="pairs",
    )(tile_count, tile_pairs.reshape(2, -1), *sources, *targets)
    partials = [partials[0]] + [
        lax.ppermute(partials[shift], "row", [(at, (at + shift) % rows) for at in range(rows)])
        for shift in range(1, rows)
    ]
    applied, stats = pl.pallas_call(
        functools.partial(sums_kernel, rows, parts),
        out_shape=[block, jax.ShapeDtypeStruct((parts, LANES), jnp.float32)],
        in_specs=[vmem] * (3 + rows),
        out_specs=[vmem] * 2,
        scratch_shapes=[pltpu.VMEM((LANES, LANES), jnp.float32)],
        compiler_params=pltpu.CompilerParams(vmem_limit_bytes=4 << 20),
        name="sums",
    )(flat_r, flat_d, noise_var.reshape(-1, LANES), *partials)
    stats = lax.all_to_all(stats, ("row", "col"), 0, 0, tiled=True)
    new_x, new_r, new_d = pl.pallas_call(
        step_kernel,
        out_shape=[flat] * 3,
        in_specs=[vmem] * 5,
        out_specs=[vmem] * 3,
        compiler_params=pltpu.CompilerParams(vmem_limit_bytes=4 << 20),
        name="step",
    )(stats, applied, flat_x, flat_r, flat_d)
    return tuple(new.reshape(direction.shape) for new in (new_x, new_r, new_d))


def solution(mesh):
    field = P(None, None, "row", "col", None)
    in_specs = (field, field, field, P(None, "row", "col", None), field, P(None, "row", "col", None), P("row", "col"))
    return jax.shard_map(
        functools.partial(per_device, mesh.shape["row"], mesh.shape["col"]),
        mesh=mesh,
        in_specs=in_specs,
        out_specs=(field, field, field),
        check_vma=False,
    )
```

```python
import functools
import jax
import jax.numpy as jnp
from jax import lax
from jax.experimental import pallas as pl
from jax.experimental.pallas import tpu as pltpu
from jax.sharding import PartitionSpec as P

EPS = 1e-06
SCALED_KERNEL = 0.125 / 256.0
TINY = 1e-30
LANES = 128
SIDES = 8
GROUP = 8


def bits_of(size):
    found = []
    bit = size // 2
    while bit:
        found.append(bit)
        bit //= 2
    return found


def masks(size):
    found = [0]
    for bit in bits_of(size):
        found = found + [mask ^ bit for mask in found]
    return found


def spread_tile(spots, slot, turned, tile, stride):
    for axis in range(3):
        for half in range(2):
            lane = axis * stride + 2 * tile + half
            spots[slot, axis, pl.ds(LANES * half, LANES), :] = jnp.broadcast_to(
                turned[:, lane : lane + 1], (LANES, LANES)
            )


def spread_kernel(owned, coords_ref, spots_ref):
    turned = 4.0 * jnp.transpose(coords_ref[...])
    for tile in range(owned):
        spread_tile(spots_ref, tile, turned, tile, 2 * owned)


def list_pairs(rows, cols, owned, count_ref, pairs_ref, tops, goals, wanted, near_row, half):
    my_row = lax.axis_index("row")
    my_col = lax.axis_index("col")
    count = count_ref[0, 0]
    lead = bits_of(cols)[:-1]
    height = (SIDES + 3) * 2 * owned
    found = jnp.int32(0)
    for slot in range(pairs_ref.shape[1]):
        row_tile = pairs_ref[0, slot]
        col_tile = pairs_ref[1, slot]
        source = lax.bitwise_xor(lax.bitwise_and(row_tile, cols - 1), my_col)
        other = lax.bitwise_and(source, 1)
        target = lax.bitwise_xor(lax.bitwise_and(col_tile, rows - 1), my_row)
        place = jnp.int32(0)
        for at, bit in enumerate(lead):
            place = place + lax.bitwise_and(lax.div(source, bit), 1) * 2**at
        kept = (slot < count) & ((target == 0) if near_row else (target != 0))
        if half is None:
            place = place + other * (cols // 2)
        else:
            kept = kept & (other == half)
        goal = lax.div(col_tile, rows)
        if not near_row:
            goal = goal + (target - 1) * owned
            wanted[jnp.where(kept, goal, (rows - 1) * owned)] = 1
        tops[found] = place * height + 2 * lax.div(row_tile, cols)
        goals[found] = goal
        found = found + kept.astype(jnp.int32)
    return found


def add_pairs(owned, found, tops, goals, stack, spots, totals):
    stride = 2 * owned
    held = SIDES * stride

    def add_pair(slot):
        top = tops[slot]
        goal = goals[slot]
        lhs_parts, near = [], []
        for side in range(2):
            values = stack[pl.ds(top + side, SIDES, stride=stride), :]
            lead = values.astype(jnp.bfloat16)
            rest = (values - lead.astype(jnp.float32)).astype(jnp.bfloat16)
            lhs_parts.append(jnp.concatenate([lead, rest], axis=0))
            near.append(
                [
                    jnp.broadcast_to(stack[pl.ds(top + held + axis * stride + side, 1), :], (16, LANES))
                    for axis in range(3)
                ]
            )
        high_parts, low_parts = [], []
        for step in range(2 * LANES // 16):
            grid = [spots[goal, axis, pl.ds(16 * step, 16), :] for axis in range(3)]
            halves_high, halves_low = [], []
            for side in range(2):
                dx = grid[0] - near[side][0]
                dy = grid[1] - near[side][1]
                dz = grid[2] - near[side][2]
                square = dx * dx + dy * dy + dz * dz
                distance = square * lax.rsqrt(jnp.maximum(square, TINY))
                left = jnp.maximum(4.0 - distance, 0.0)
                left = left * left
                weight = left * left * (distance + 1.0)
                high = weight.astype(jnp.bfloat16)
                halves_high.append(high)
                halves_low.append((weight - high.astype(jnp.float32)).astype(jnp.bfloat16))
            high_parts.append(jnp.concatenate(halves_high, axis=1))
            low_parts.append(jnp.concatenate(halves_low, axis=1))
        lhs = jnp.concatenate(lhs_parts, axis=1)
        dims = (((1,), (1,)), ((), ()))
        product = lax.dot_general(
            lhs, jnp.concatenate(high_parts, axis=0), dims, preferred_element_type=jnp.float32
        ) + lax.dot_general(
            lhs, jnp.concatenate(low_parts, axis=0), dims, preferred_element_type=jnp.float32
        )
        summed = product[:SIDES] + product[SIDES:]
        for half in range(2):
            totals[2 * goal + half] += summed[:, LANES * half : LANES * half + LANES]

    whole = lax.div(found, GROUP)

    def add_group(step, carry):
        for part in range(GROUP):
            add_pair(GROUP * step + part)
        return carry

    def add_one(slot, carry):
        add_pair(slot)
        return carry

    lax.fori_loop(0, whole, add_group, jnp.int32(0))
    lax.fori_loop(GROUP * whole, found, add_one, jnp.int32(0))


def near_kernel(rows, cols, owned, half, count_ref, pairs_ref, stack, spots, totals, tops, goals):
    totals[...] = jnp.zeros_like(totals)
    found = list_pairs(
        rows, cols, owned, count_ref, pairs_ref, tops, goals, None, True, half
    )
    add_pairs(owned, found, tops, goals, stack, spots, totals)


def far_kernel(rows, cols, owned, count_ref, pairs_ref, *refs):
    stacks = refs[:2]
    points = refs[2:4]
    outs = refs[4 : 3 + rows]
    slab, spots, totals, tops, goals, wanted = refs[3 + rows :]
    stride = 2 * owned
    spread = 3 * stride
    for tile in range((rows - 1) * owned):
        wanted[tile] = 0
    found = list_pairs(
        rows, cols, owned, count_ref, pairs_ref, tops, goals, wanted, False, None
    )
    totals[...] = jnp.zeros_like(totals)

    @pl.when(found > 0)
    def _():
        span = stacks[0].shape[0]
        slab[pl.ds(0, span), :] = stacks[0][...]
        slab[pl.ds(span, span), :] = stacks[1][...]
        for place, mask in enumerate(masks(rows)):
            if mask:
                top = (place % (rows // 2)) * spread
                turned = 4.0 * jnp.transpose(points[place // (rows // 2)][pl.ds(top, spread), :])
                for tile in range(owned):
                    slot = (mask - 1) * owned + tile

                    @pl.when(wanted[slot] == 1)
                    def _():
                        spread_tile(spots, slot, turned, tile, stride)

        add_pairs(owned, found, tops, goals, slab, spots, totals)

    for at in range(rows - 1):
        outs[at][...] = totals[pl.ds(at * stride, stride)]


def sums_kernel(terms, residual_ref, direction_ref, noise_ref, *refs):
    partials = refs[:terms]
    applied_ref, stats_ref, stack = refs[terms:]
    halves = noise_ref.shape[0]
    zero = jnp.zeros((SIDES, LANES), jnp.float32)
    now, bend, cross, size = zero, zero, zero, zero
    for part in range(halves):
        total = partials[0][part]
        for other in partials[1:]:
            total = total + other[part]
        residual = residual_ref[pl.ds(part, SIDES, stride=halves), :]
        direction = direction_ref[pl.ds(part, SIDES, stride=halves), :]
        applied = noise_ref[part : part + 1, :] * direction + SCALED_KERNEL * total
        applied_ref[part] = applied
        now = now + residual * residual
        bend = bend + direction * applied
        cross = cross + residual * applied
        size = size + applied * applied
    stack[...] = jnp.zeros_like(stack)
    for slot, value in enumerate((now, bend, cross, size)):
        stack[SIDES * slot : SIDES * slot + SIDES, :] = value
    stats_ref[...] = lax.dot_general(
        jnp.ones((stats_ref.shape[0], LANES), jnp.float32),
        stack[...],
        (((1,), (1,)), ((), ())),
        precision=lax.Precision.HIGHEST,
        preferred_element_type=jnp.float32,
    )


def step_kernel(
    stats_ref, applied_ref, solution_ref, residual_ref, direction_ref, new_x, new_r, new_d
):
    halves = applied_ref.shape[0]
    summed = jnp.sum(stats_ref[...], axis=0, keepdims=True)
    summed = jnp.broadcast_to(summed, (SIDES, LANES))
    lane = lax.broadcasted_iota(jnp.int32, (SIDES, LANES), 1)
    line = lax.broadcasted_iota(jnp.int32, (SIDES, LANES), 0)

    def pick(slot):
        return jnp.sum(
            jnp.where(lane == line + SIDES * slot, summed, 0.0), axis=1, keepdims=True
        )

    now, bend, cross, size = pick(0), pick(1), pick(2), pick(3)
    step = now / bend
    after = jnp.maximum(now - 2.0 * step * cross + step * step * size, 0.0)
    beta = jnp.broadcast_to(after / (now + EPS), (SIDES, LANES))
    step = jnp.broadcast_to(step, (SIDES, LANES))
    for part in range(halves):
        place = pl.ds(part, SIDES, stride=halves)
        direction = direction_ref[place, :]
        new_x[place, :] = solution_ref[place, :] + step * direction
        residual = residual_ref[place, :] - step * applied_ref[part]
        new_r[place, :] = residual
        new_d[place, :] = residual + beta * direction


def per_device(rows, cols, solution, residual, direction, noise_var, coords, tile_pairs, tile_count):
    sides, owned, _, _, tile_size = direction.shape
    assert sides == SIDES and tile_size == 2 * LANES
    assert rows & (rows - 1) == 0 and cols & (cols - 1) == 0 and rows > 1 and cols > 1
    parts = rows * cols
    halves = 2 * owned
    flat_x = solution.reshape(-1, LANES)
    flat_r = residual.reshape(-1, LANES)
    flat_d = direction.reshape(-1, LANES)
    flat_c = coords.reshape(-1, LANES)
    pairs = tile_pairs.reshape(2, -1)
    slots = pairs.shape[1] + 1
    vmem = pl.BlockSpec(memory_space=pltpu.VMEM)
    smem = pl.BlockSpec(memory_space=pltpu.SMEM)
    block = jax.ShapeDtypeStruct((halves, sides, LANES), jnp.float32)
    flat = jax.ShapeDtypeStruct(flat_d.shape, jnp.float32)
    lists = [pltpu.SMEM((slots,), jnp.int32)] * 2

    def hop(value, axis, size, bit):
        return lax.ppermute(value, axis, [(at, at ^ bit) for at in range(size)])

    spots = pl.pallas_call(
        functools.partial(spread_kernel, owned),
        out_shape=jax.ShapeDtypeStruct((owned, 3, tile_size, LANES), jnp.float32),
        in_specs=[vmem],
        out_specs=vmem,
        compiler_params=pltpu.CompilerParams(vmem_limit_bytes=8 << 20),
        cost_estimate=pl.CostEstimate(flops=10**9, bytes_accessed=10**5, transcendentals=0),
        name="spread",
    )(flat_c)

    held_s = jnp.concatenate([flat_d, 4.0 * flat_c], axis=0)
    held_c = flat_c
    bits_s, bits_c = bits_of(cols), bits_of(rows)
    while len(bits_s) > 1 or len(bits_c) > 1:
        moved_s = moved_c = None
        if len(bits_s) > 1:
            moved_s = hop(held_s, "col", cols, bits_s[0])
        if len(bits_c) > 1:
            moved_c = hop(held_c, "row", rows, bits_c[0])
        moved_s, moved_c = lax.optimization_barrier((moved_s, moved_c))
        if moved_s is not None:
            held_s = jnp.concatenate([held_s, moved_s], axis=0)
            bits_s = bits_s[1:]
        if moved_c is not None:
            held_c = jnp.concatenate([held_c, moved_c], axis=0)
            bits_c = bits_c[1:]
    moved_s = hop(held_s, "col", cols, bits_s[0])
    moved_c = hop(held_c, "row", rows, bits_c[0])

    def near(half, stack):
        return pl.pallas_call(
            functools.partial(near_kernel, rows, cols, owned, half),
            out_shape=block,
            in_specs=[smem, smem, vmem, vmem],
            out_specs=vmem,
            scratch_shapes=lists,
            compiler_params=pltpu.CompilerParams(vmem_limit_bytes=16 << 20),
            cost_estimate=pl.CostEstimate(flops=10**10, bytes_accessed=10**6, transcendentals=0),
            name="near",
        )(tile_count, pairs, stack, spots)

    total_first = near(0, held_s)
    total_first, moved_s, moved_c = lax.optimization_barrier((total_first, moved_s, moved_c))
    partials = pl.pallas_call(
        functools.partial(far_kernel, rows, cols, owned),
        out_shape=[block] * (rows - 1),
        in_specs=[smem, smem] + [vmem] * 4,
        out_specs=[vmem] * (rows - 1),
        scratch_shapes=[
            pltpu.VMEM((2 * held_s.shape[0], LANES), jnp.float32),
            pltpu.VMEM(((rows - 1) * owned, 3, tile_size, LANES), jnp.float32),
            pltpu.VMEM(((rows - 1) * halves, sides, LANES), jnp.float32),
        ]
        + lists
        + [pltpu.SMEM(((rows - 1) * owned + 1,), jnp.int32)],
        compiler_params=pltpu.CompilerParams(vmem_limit_bytes=36 << 20),
        cost_estimate=pl.CostEstimate(flops=10**10, bytes_accessed=10**6, transcendentals=0),
        name="far",
    )(tile_count, pairs, held_s, moved_s, held_c, moved_c)
    *partials, moved_s = lax.optimization_barrier((*partials, moved_s))
    arrived = [hop(partials[mask - 1], "row", rows, mask) for mask in range(1, rows)]
    total_last = near(1, moved_s)
    *arrived, total_last = lax.optimization_barrier((*arrived, total_last))
    terms = [total_first, total_last] + arrived
    applied, stats = pl.pallas_call(
        functools.partial(sums_kernel, len(terms)),
        out_shape=[block, jax.ShapeDtypeStruct((parts, LANES), jnp.float32)],
        in_specs=[vmem] * (3 + len(terms)),
        out_specs=[vmem] * 2,
        scratch_shapes=[pltpu.VMEM((LANES, LANES), jnp.float32)],
        compiler_params=pltpu.CompilerParams(vmem_limit_bytes=4 << 20),
        name="sums",
    )(flat_r, flat_d, noise_var.reshape(-1, LANES), *terms)
    stats = lax.all_to_all(stats, ("row", "col"), 0, 0, tiled=True)
    new_x, new_r, new_d = pl.pallas_call(
        step_kernel,
        out_shape=[flat] * 3,
        in_specs=[vmem] * 5,
        out_specs=[vmem] * 3,
        compiler_params=pltpu.CompilerParams(vmem_limit_bytes=4 << 20),
        name="step",
    )(stats, applied, flat_x, flat_r, flat_d)
    return tuple(new.reshape(direction.shape) for new in (new_x, new_r, new_d))


def solution(mesh):
    field = P(None, None, "row", "col", None)
    in_specs = (
        field,
        field,
        field,
        P(None, "row", "col", None),
        field,
        P(None, "row", "col", None),
        P("row", "col"),
    )
    return jax.shard_map(
        functools.partial(per_device, mesh.shape["row"], mesh.shape["col"]),
        mesh=mesh,
        in_specs=in_specs,
        out_specs=(field, field, field),
        check_vma=False,
    )
```

```python
import functools
import jax
import jax.numpy as jnp
from jax import lax
from jax.experimental import pallas as pl
from jax.experimental.pallas import tpu as pltpu
from jax.sharding import PartitionSpec as P

EPS = 1e-06
SCALED_KERNEL = 0.125 / 256.0
TINY = 1e-30
LANES = 128
SIDES = 8
GROUP = 8


def bits_of(size):
    found = []
    bit = size // 2
    while bit:
        found.append(bit)
        bit //= 2
    return found


def masks(size):
    found = [0]
    for bit in bits_of(size):
        found = found + [mask ^ bit for mask in found]
    return found


def spread_tile(spots, slot, turned, tile, stride):
    for axis in range(3):
        for half in range(2):
            lane = axis * stride + 2 * tile + half
            spots[slot, axis, pl.ds(LANES * half, LANES), :] = jnp.broadcast_to(
                turned[:, lane : lane + 1], (LANES, LANES)
            )


def plan_kernel(rows, cols, owned, count_ref, pairs_ref, coords_ref, spots_ref, lists):
    my_row = lax.axis_index("row")
    my_col = lax.axis_index("col")
    bits = bits_of(cols)[:-1]
    stages = len(bits)
    far = 2 * stages
    height = (SIDES + 3) * 2 * owned
    slots = pairs_ref.shape[1]
    for at in range(far + 1):
        lists[at] = 0

    def sort_pair(slot, carry):
        row_tile = pairs_ref[0, slot]
        col_tile = pairs_ref[1, slot]
        source = lax.bitwise_xor(lax.bitwise_and(row_tile, cols - 1), my_col)
        target = lax.bitwise_xor(lax.bitwise_and(col_tile, rows - 1), my_row)
        core = lax.bitwise_and(source, 1)
        goal = lax.div(col_tile, rows)
        place = lax.bitwise_and(lax.div(source, bits[0]), 1)
        near_place = place
        group = jnp.int32(0)
        for at in range(1, stages):
            here = lax.bitwise_and(lax.div(source, bits[at]), 1)
            group = jnp.where(here == 1, at, group)
            near_place = jnp.where(here == 1, place, near_place)
            place = place + here * 2**at
        is_near = target == 0
        group = jnp.where(is_near, group + core * stages, far)
        place = jnp.where(is_near, near_place, place + core * (cols // 2))
        goal = jnp.where(is_near, goal, goal + (target - 1) * owned)
        found = lists[group]
        entry = far + 1 + 2 * (group * slots + found)
        lists[entry] = place * height + 2 * lax.div(row_tile, cols)
        lists[entry + 1] = goal
        lists[group] = found + 1
        return carry

    lax.fori_loop(0, count_ref[0, 0], sort_pair, jnp.int32(0))
    turned = 4.0 * jnp.transpose(coords_ref[...])
    for tile in range(owned):
        spread_tile(spots_ref, tile, turned, tile, 2 * owned)


def add_pairs(owned, found, base, lists, stack, spots, totals):
    stride = 2 * owned
    held = SIDES * stride

    def add_pair(slot):
        top = lists[base + 2 * slot]
        goal = lists[base + 2 * slot + 1]
        lhs_parts, near = [], []
        for side in range(2):
            values = stack[pl.ds(top + side, SIDES, stride=stride), :]
            lead = values.astype(jnp.bfloat16)
            rest = (values - lead.astype(jnp.float32)).astype(jnp.bfloat16)
            lhs_parts.append(jnp.concatenate([lead, rest], axis=0))
            near.append(
                [
                    jnp.broadcast_to(4.0 * stack[pl.ds(top + held + axis * stride + side, 1), :], (16, LANES))
                    for axis in range(3)
                ]
            )
        high_parts, low_parts = [], []
        for step in range(2 * LANES // 16):
            grid = [spots[goal, axis, pl.ds(16 * step, 16), :] for axis in range(3)]
            halves_high, halves_low = [], []
            for side in range(2):
                dx = grid[0] - near[side][0]
                dy = grid[1] - near[side][1]
                dz = grid[2] - near[side][2]
                square = dx * dx + dy * dy + dz * dz
                distance = square * lax.rsqrt(jnp.maximum(square, TINY))
                left = jnp.maximum(4.0 - distance, 0.0)
                left = left * left
                weight = left * left * (distance + 1.0)
                high = weight.astype(jnp.bfloat16)
                halves_high.append(high)
                halves_low.append((weight - high.astype(jnp.float32)).astype(jnp.bfloat16))
            high_parts.append(jnp.concatenate(halves_high, axis=1))
            low_parts.append(jnp.concatenate(halves_low, axis=1))
        lhs = jnp.concatenate(lhs_parts, axis=1)
        dims = (((1,), (1,)), ((), ()))
        product = lax.dot_general(
            lhs, jnp.concatenate(high_parts, axis=0), dims, preferred_element_type=jnp.float32
        ) + lax.dot_general(
            lhs, jnp.concatenate(low_parts, axis=0), dims, preferred_element_type=jnp.float32
        )
        summed = product[:SIDES] + product[SIDES:]
        for half in range(2):
            totals[2 * goal + half] += summed[:, LANES * half : LANES * half + LANES]

    whole = lax.div(found, GROUP)

    def add_group(step, carry):
        for part in range(GROUP):
            add_pair(GROUP * step + part)
        return carry

    def add_one(slot, carry):
        add_pair(slot)
        return carry

    lax.fori_loop(0, whole, add_group, jnp.int32(0))
    lax.fori_loop(GROUP * whole, found, add_one, jnp.int32(0))


def near_kernel(owned, groups, far, slots, lists, spots, *refs):
    totals = refs[-1]
    totals[...] = jnp.zeros_like(totals)
    for group, stack in zip(groups, refs):
        base = far + 1 + 2 * group * slots
        add_pairs(owned, lists[group], base, lists, stack, spots, totals)


def far_kernel(rows, owned, far, slots, lists, *refs):
    points = refs[:2]
    stacks = refs[2 : 2 + far]
    outs = refs[2 + far : 1 + far + rows]
    slab, spots, totals, wanted = refs[1 + far + rows :]
    stride = 2 * owned
    spread = 3 * stride
    found = lists[far]
    base = far + 1 + 2 * far * slots

    @pl.when(found == 0)
    def _():
        for out in outs:
            out[...] = jnp.zeros_like(out)

    @pl.when(found > 0)
    def _():
        for tile in range((rows - 1) * owned):
            wanted[tile] = 0

        def want(slot, carry):
            wanted[lists[base + 2 * slot + 1]] = 1
            return carry

        lax.fori_loop(0, found, want, jnp.int32(0))
        totals[...] = jnp.zeros_like(totals)
        top = 0
        for stack in stacks:
            slab[pl.ds(top, stack.shape[0]), :] = stack[...]
            top += stack.shape[0]
        for place, mask in enumerate(masks(rows)):
            if mask:
                top = (place % (rows // 2)) * spread
                turned = 4.0 * jnp.transpose(points[place // (rows // 2)][pl.ds(top, spread), :])
                for tile in range(owned):
                    slot = (mask - 1) * owned + tile

                    @pl.when(wanted[slot] == 1)
                    def _():
                        spread_tile(spots, slot, turned, tile, stride)

        add_pairs(owned, found, base, lists, slab, spots, totals)
        for at in range(rows - 1):
            outs[at][...] = totals[pl.ds(at * stride, stride)]


def sums_kernel(terms, residual_ref, direction_ref, noise_ref, *refs):
    partials = refs[:terms]
    applied_ref, stats_ref, stack = refs[terms:]
    halves = noise_ref.shape[0]
    zero = jnp.zeros((SIDES, LANES), jnp.float32)
    now, bend, cross, size = zero, zero, zero, zero
    for part in range(halves):
        total = partials[0][part]
        for other in partials[1:]:
            total = total + other[part]
        residual = residual_ref[pl.ds(part, SIDES, stride=halves), :]
        direction = direction_ref[pl.ds(part, SIDES, stride=halves), :]
        applied = noise_ref[part : part + 1, :] * direction + SCALED_KERNEL * total
        applied_ref[part] = applied
        now = now + residual * residual
        bend = bend + direction * applied
        cross = cross + residual * applied
        size = size + applied * applied
    stack[...] = jnp.zeros_like(stack)
    for slot, value in enumerate((now, bend, cross, size)):
        stack[SIDES * slot : SIDES * slot + SIDES, :] = value
    stats_ref[...] = lax.dot_general(
        jnp.ones((stats_ref.shape[0], LANES), jnp.float32),
        stack[...],
        (((1,), (1,)), ((), ())),
        precision=lax.Precision.HIGHEST,
        preferred_element_type=jnp.float32,
    )


def step_kernel(
    stats_ref, applied_ref, solution_ref, residual_ref, direction_ref, new_x, new_r, new_d
):
    halves = applied_ref.shape[0]
    summed = jnp.sum(stats_ref[...], axis=0, keepdims=True)
    summed = jnp.broadcast_to(summed, (SIDES, LANES))
    lane = lax.broadcasted_iota(jnp.int32, (SIDES, LANES), 1)
    line = lax.broadcasted_iota(jnp.int32, (SIDES, LANES), 0)

    def pick(slot):
        return jnp.sum(
            jnp.where(lane == line + SIDES * slot, summed, 0.0), axis=1, keepdims=True
        )

    now, bend, cross, size = pick(0), pick(1), pick(2), pick(3)
    step = now / bend
    after = jnp.maximum(now - 2.0 * step * cross + step * step * size, 0.0)
    beta = jnp.broadcast_to(after / (now + EPS), (SIDES, LANES))
    step = jnp.broadcast_to(step, (SIDES, LANES))
    for part in range(halves):
        place = pl.ds(part, SIDES, stride=halves)
        direction = direction_ref[place, :]
        new_x[place, :] = solution_ref[place, :] + step * direction
        residual = residual_ref[place, :] - step * applied_ref[part]
        new_r[place, :] = residual
        new_d[place, :] = residual + beta * direction


def per_device(rows, cols, solution, residual, direction, noise_var, coords, tile_pairs, tile_count):
    sides, owned, _, _, tile_size = direction.shape
    assert sides == SIDES and tile_size == 2 * LANES
    assert rows & (rows - 1) == 0 and cols & (cols - 1) == 0 and cols >= rows > 1 and cols > 2
    parts = rows * cols
    halves = 2 * owned
    flat_x = solution.reshape(-1, LANES)
    flat_r = residual.reshape(-1, LANES)
    flat_d = direction.reshape(-1, LANES)
    flat_c = coords.reshape(-1, LANES)
    pairs = tile_pairs.reshape(2, -1)
    slots = pairs.shape[1]
    vmem = pl.BlockSpec(memory_space=pltpu.VMEM)
    smem = pl.BlockSpec(memory_space=pltpu.SMEM)
    block = jax.ShapeDtypeStruct((halves, sides, LANES), jnp.float32)
    flat = jax.ShapeDtypeStruct(flat_d.shape, jnp.float32)

    def hop(value, axis, size, bit):
        return lax.ppermute(value, axis, [(at, at ^ bit) for at in range(size)])

    bits_s, bits_c = bits_of(cols)[:-1], bits_of(rows)
    stages = len(bits_s)
    assert stages >= len(bits_c) - 1
    far = 2 * stages
    spots, lists = pl.pallas_call(
        functools.partial(plan_kernel, rows, cols, owned),
        out_shape=[
            jax.ShapeDtypeStruct((owned, 3, tile_size, LANES), jnp.float32),
            jax.ShapeDtypeStruct(((far + 1) * (2 * slots + 1) + 1,), jnp.int32),
        ],
        in_specs=[smem, smem, vmem],
        out_specs=[vmem, smem],
        compiler_params=pltpu.CompilerParams(vmem_limit_bytes=8 << 20),
        cost_estimate=pl.CostEstimate(flops=10**9, bytes_accessed=10**5, transcendentals=0),
        name="plan",
    )(tile_count, pairs, flat_c)

    def near(groups, stacks):
        return pl.pallas_call(
            functools.partial(near_kernel, owned, groups, far, slots),
            out_shape=block,
            in_specs=[smem] + [vmem] * (1 + len(stacks)),
            out_specs=vmem,
            compiler_params=pltpu.CompilerParams(vmem_limit_bytes=16 << 20),
            cost_estimate=pl.CostEstimate(flops=10**10, bytes_accessed=10**6, transcendentals=0),
            name="near",
        )(lists, spots, *stacks)

    moved = [hop(flat_d, "col", cols, bits_s[0]), hop(flat_c, "col", cols, bits_s[0])]
    held_c = flat_c
    moved_c = hop(held_c, "row", rows, bits_c[0])
    *moved, moved_c = lax.optimization_barrier((*moved, moved_c))
    stacks = [lax.optimization_barrier(jnp.concatenate([flat_d, flat_c] + moved, axis=0))]
    swapped, terms = [], []
    for at in range(stages):
        fresh = None
        if at < stages - 1:
            sent = stacks[0] if at == 0 else jnp.concatenate(stacks, axis=0)
            fresh = hop(sent, "col", cols, bits_s[at + 1])
        if at + 1 < len(bits_c):
            held_c = jnp.concatenate([held_c, moved_c], axis=0)
            moved_c = hop(held_c, "row", rows, bits_c[at + 1])
        swapped.append(hop(stacks[at], "col", cols, 1))
        term = near([0], [stacks[0]]) if at == 0 else near([stages + at - 1], [swapped[at - 1]])
        if fresh is None:
            term, swapped[at], moved_c = lax.optimization_barrier((term, swapped[at], moved_c))
        else:
            term, fresh, moved_c = lax.optimization_barrier((term, fresh, moved_c))
            stacks.append(fresh)
        terms.append(term)
    heights = sum(stack.shape[0] for stack in stacks + swapped)
    partials = pl.pallas_call(
        functools.partial(far_kernel, rows, owned, far, slots),
        out_shape=[block] * (rows - 1),
        in_specs=[smem] + [vmem] * (2 + far),
        out_specs=[vmem] * (rows - 1),
        scratch_shapes=[
            pltpu.VMEM((heights, LANES), jnp.float32),
            pltpu.VMEM(((rows - 1) * owned, 3, tile_size, LANES), jnp.float32),
            pltpu.VMEM(((rows - 1) * halves, sides, LANES), jnp.float32),
            pltpu.SMEM(((rows - 1) * owned,), jnp.int32),
        ],
        compiler_params=pltpu.CompilerParams(vmem_limit_bytes=36 << 20),
        cost_estimate=pl.CostEstimate(flops=10**10, bytes_accessed=10**6, transcendentals=0),
        name="far",
    )(lists, held_c, moved_c, *stacks, *swapped)
    late = stacks[1:] + swapped[-1:]
    *partials, spots = lax.optimization_barrier((*partials, spots))
    arrived = [hop(partials[mask - 1], "row", rows, mask) for mask in range(1, rows)]
    terms.append(near(list(range(1, stages)) + [far - 1], late))
    *arrived, terms[-1] = lax.optimization_barrier((*arrived, terms[-1]))
    terms = terms + arrived
    applied, stats = pl.pallas_call(
        functools.partial(sums_kernel, len(terms)),
        out_shape=[block, jax.ShapeDtypeStruct((parts, LANES), jnp.float32)],
        in_specs=[vmem] * (3 + len(terms)),
        out_specs=[vmem] * 2,
        scratch_shapes=[pltpu.VMEM((LANES, LANES), jnp.float32)],
        compiler_params=pltpu.CompilerParams(vmem_limit_bytes=4 << 20),
        name="sums",
    )(flat_r, flat_d, noise_var.reshape(-1, LANES), *terms)
    stats = lax.all_to_all(stats, ("row", "col"), 0, 0, tiled=True)
    new_x, new_r, new_d = pl.pallas_call(
        step_kernel,
        out_shape=[flat] * 3,
        in_specs=[vmem] * 5,
        out_specs=[vmem] * 3,
        compiler_params=pltpu.CompilerParams(vmem_limit_bytes=4 << 20),
        name="step",
    )(stats, applied, flat_x, flat_r, flat_d)
    return tuple(new.reshape(direction.shape) for new in (new_x, new_r, new_d))


def solution(mesh):
    field = P(None, None, "row", "col", None)
    in_specs = (
        field,
        field,
        field,
        P(None, "row", "col", None),
        field,
        P(None, "row", "col", None),
        P("row", "col"),
    )
    return jax.shard_map(
        functools.partial(per_device, mesh.shape["row"], mesh.shape["col"]),
        mesh=mesh,
        in_specs=in_specs,
        out_specs=(field, field, field),
        check_vma=False,
    )
```

```python
import functools
import jax
import jax.numpy as jnp
from jax import lax
from jax.experimental import pallas as pl
from jax.experimental.pallas import tpu as pltpu
from jax.sharding import PartitionSpec as P

EPS = 1e-06
SCALED_KERNEL = 0.125 / 256.0
TINY = 1e-30
LANES = 128
SIDES = 8
GROUP = 8


def bits_of(size):
    found = []
    bit = size // 2
    while bit:
        found.append(bit)
        bit //= 2
    return found


def masks(size):
    found = [0]
    for bit in bits_of(size):
        found = found + [mask ^ bit for mask in found]
    return found


def spread_tile(spots, slot, turned, tile, stride):
    for axis in range(3):
        for half in range(2):
            lane = axis * stride + 2 * tile + half
            spots[slot, axis, pl.ds(LANES * half, LANES), :] = jnp.broadcast_to(
                turned[:, lane : lane + 1], (LANES, LANES)
            )


def plan_kernel(
    rows, cols, owned, count, pairs_hbm, coords_hbm, spots_ref, lists, pairs, coords, tally, sems
):
    copies = [
        pltpu.make_async_copy(source, target, sems.at[at])
        for at, (source, target) in enumerate(
            ((pairs_hbm, pairs), (coords_hbm, coords))
        )
    ]
    for copy in copies:
        copy.start()
    my_row = lax.axis_index("row")
    my_col = lax.axis_index("col")
    bits = bits_of(cols)[:-1]
    stages = len(bits)
    far = 2 * stages
    height = (SIDES + 3) * 2 * owned
    slots = pairs.shape[1]
    col_shift = cols.bit_length() - 1
    row_shift = rows.bit_length() - 1
    for at in range(far + 1):
        tally[at] = 0
    for copy in copies:
        copy.wait()
    live = count[0, 0]
    for slot in range(slots):
        row_tile = pairs[0, slot]
        col_tile = pairs[1, slot]
        source = lax.bitwise_xor(row_tile & (cols - 1), my_col)
        target = lax.bitwise_xor(col_tile & (rows - 1), my_row)
        core = source & 1
        goal = lax.shift_right_logical(col_tile, row_shift)
        place = lax.shift_right_logical(source, bits[0].bit_length() - 1) & 1
        near_place = place
        group = jnp.int32(0)
        for at in range(1, stages):
            here = lax.shift_right_logical(source, bits[at].bit_length() - 1) & 1
            group = jnp.where(here == 1, at, group)
            near_place = jnp.where(here == 1, place, near_place)
            place = place + here * 2**at
        is_near = target == 0
        group = jnp.where(is_near, group + core * stages, far)
        place = jnp.where(is_near, near_place, place + core * (cols // 2))
        goal = jnp.where(is_near, goal, goal + (target - 1) * owned)
        found = tally[group]
        entry = far + 1 + 2 * (group * slots + found)
        lists[entry] = place * height + 2 * lax.shift_right_logical(row_tile, col_shift)
        lists[entry + 1] = goal
        tally[group] = found + (slot < live).astype(jnp.int32)
    for at in range(far + 1):
        lists[at] = tally[at]
    turned = 4.0 * jnp.transpose(coords[...])
    for tile in range(owned):
        spread_tile(spots_ref, tile, turned, tile, 2 * owned)


def add_pairs(owned, found, base, lists, stack, spots, totals):
    stride = 2 * owned
    held = SIDES * stride

    def add_pair(slot):
        top = lists[base + 2 * slot]
        goal = lists[base + 2 * slot + 1]
        lhs_parts, near = [], []
        for side in range(2):
            values = stack[pl.ds(top + side, SIDES, stride=stride), :]
            lead = values.astype(jnp.bfloat16)
            rest = (values - lead.astype(jnp.float32)).astype(jnp.bfloat16)
            lhs_parts.append(jnp.concatenate([lead, rest], axis=0))
            near.append(
                [
                    jnp.broadcast_to(4.0 * stack[pl.ds(top + held + axis * stride + side, 1), :], (16, LANES))
                    for axis in range(3)
                ]
            )
        high_parts, low_parts = [], []
        for step in range(2 * LANES // 16):
            grid = [spots[goal, axis, pl.ds(16 * step, 16), :] for axis in range(3)]
            halves_high, halves_low = [], []
            for side in range(2):
                dx = grid[0] - near[side][0]
                dy = grid[1] - near[side][1]
                dz = grid[2] - near[side][2]
                square = dx * dx + dy * dy + dz * dz
                distance = square * lax.rsqrt(jnp.maximum(square, TINY))
                left = jnp.maximum(4.0 - distance, 0.0)
                left = left * left
                weight = left * left * (distance + 1.0)
                high = weight.astype(jnp.bfloat16)
                halves_high.append(high)
                halves_low.append((weight - high.astype(jnp.float32)).astype(jnp.bfloat16))
            high_parts.append(jnp.concatenate(halves_high, axis=1))
            low_parts.append(jnp.concatenate(halves_low, axis=1))
        lhs = jnp.concatenate(lhs_parts, axis=1)
        dims = (((1,), (1,)), ((), ()))
        product = lax.dot_general(
            lhs, jnp.concatenate(high_parts, axis=0), dims, preferred_element_type=jnp.float32
        ) + lax.dot_general(
            lhs, jnp.concatenate(low_parts, axis=0), dims, preferred_element_type=jnp.float32
        )
        summed = product[:SIDES] + product[SIDES:]
        for half in range(2):
            totals[2 * goal + half] += summed[:, LANES * half : LANES * half + LANES]

    whole = lax.div(found, GROUP)

    def add_group(step, carry):
        for part in range(GROUP):
            add_pair(GROUP * step + part)
        return carry

    def add_one(slot, carry):
        add_pair(slot)
        return carry

    lax.fori_loop(0, whole, add_group, jnp.int32(0))
    lax.fori_loop(GROUP * whole, found, add_one, jnp.int32(0))


def near_kernel(owned, groups, far, slots, lists, spots, *refs):
    totals = refs[-1]
    totals[...] = jnp.zeros_like(totals)
    for group, stack in zip(groups, refs):
        base = far + 1 + 2 * group * slots
        add_pairs(owned, lists[group], base, lists, stack, spots, totals)


def far_kernel(rows, owned, far, slots, lists, *refs):
    points = refs[:2]
    stacks = refs[2 : 2 + far]
    outs = refs[2 + far : 1 + far + rows]
    slab, spots, totals, wanted = refs[1 + far + rows :]
    stride = 2 * owned
    spread = 3 * stride
    found = lists[far]
    base = far + 1 + 2 * far * slots

    @pl.when(found == 0)
    def _():
        for out in outs:
            out[...] = jnp.zeros_like(out)

    @pl.when(found > 0)
    def _():
        for tile in range((rows - 1) * owned):
            wanted[tile] = 0

        def want(slot, carry):
            wanted[lists[base + 2 * slot + 1]] = 1
            return carry

        lax.fori_loop(0, found, want, jnp.int32(0))
        totals[...] = jnp.zeros_like(totals)
        top = 0
        for stack in stacks:
            slab[pl.ds(top, stack.shape[0]), :] = stack[...]
            top += stack.shape[0]
        for place, mask in enumerate(masks(rows)):
            if mask:
                top = (place % (rows // 2)) * spread
                turned = 4.0 * jnp.transpose(points[place // (rows // 2)][pl.ds(top, spread), :])
                for tile in range(owned):
                    slot = (mask - 1) * owned + tile

                    @pl.when(wanted[slot] == 1)
                    def _():
                        spread_tile(spots, slot, turned, tile, stride)

        add_pairs(owned, found, base, lists, slab, spots, totals)
        for at in range(rows - 1):
            outs[at][...] = totals[pl.ds(at * stride, stride)]


def sums_kernel(terms, residual_ref, direction_ref, noise_ref, *refs):
    partials = refs[:terms]
    applied_ref, stats_ref, stack = refs[terms:]
    halves = noise_ref.shape[0]
    zero = jnp.zeros((SIDES, LANES), jnp.float32)
    now, bend, cross, size = zero, zero, zero, zero
    for part in range(halves):
        total = partials[0][part]
        for other in partials[1:]:
            total = total + other[part]
        residual = residual_ref[pl.ds(part, SIDES, stride=halves), :]
        direction = direction_ref[pl.ds(part, SIDES, stride=halves), :]
        applied = noise_ref[part : part + 1, :] * direction + SCALED_KERNEL * total
        applied_ref[part] = applied
        now = now + residual * residual
        bend = bend + direction * applied
        cross = cross + residual * applied
        size = size + applied * applied
    stack[...] = jnp.zeros_like(stack)
    for slot, value in enumerate((now, bend, cross, size)):
        stack[SIDES * slot : SIDES * slot + SIDES, :] = value
    stats_ref[...] = lax.dot_general(
        jnp.ones((stats_ref.shape[0], LANES), jnp.float32),
        stack[...],
        (((1,), (1,)), ((), ())),
        precision=lax.Precision.HIGHEST,
        preferred_element_type=jnp.float32,
    )


def step_kernel(
    stats_ref, applied_ref, solution_ref, residual_ref, direction_ref, new_x, new_r, new_d
):
    halves = applied_ref.shape[0]
    summed = jnp.sum(stats_ref[...], axis=0, keepdims=True)
    summed = jnp.broadcast_to(summed, (SIDES, LANES))
    lane = lax.broadcasted_iota(jnp.int32, (SIDES, LANES), 1)
    line = lax.broadcasted_iota(jnp.int32, (SIDES, LANES), 0)

    def pick(slot):
        return jnp.sum(
            jnp.where(lane == line + SIDES * slot, summed, 0.0), axis=1, keepdims=True
        )

    now, bend, cross, size = pick(0), pick(1), pick(2), pick(3)
    step = now / bend
    after = jnp.maximum(now - 2.0 * step * cross + step * step * size, 0.0)
    beta = jnp.broadcast_to(after / (now + EPS), (SIDES, LANES))
    step = jnp.broadcast_to(step, (SIDES, LANES))
    for part in range(halves):
        place = pl.ds(part, SIDES, stride=halves)
        direction = direction_ref[place, :]
        new_x[place, :] = solution_ref[place, :] + step * direction
        residual = residual_ref[place, :] - step * applied_ref[part]
        new_r[place, :] = residual
        new_d[place, :] = residual + beta * direction


def per_device(rows, cols, solution, residual, direction, noise_var, coords, tile_pairs, tile_count):
    sides, owned, _, _, tile_size = direction.shape
    assert sides == SIDES and tile_size == 2 * LANES
    assert rows & (rows - 1) == 0 and cols & (cols - 1) == 0 and cols >= rows > 1 and cols > 2
    parts = rows * cols
    halves = 2 * owned
    flat_x = solution.reshape(-1, LANES)
    flat_r = residual.reshape(-1, LANES)
    flat_d = direction.reshape(-1, LANES)
    flat_c = coords.reshape(-1, LANES)
    pairs = tile_pairs.reshape(2, -1)
    slots = pairs.shape[1]
    vmem = pl.BlockSpec(memory_space=pltpu.VMEM)
    smem = pl.BlockSpec(memory_space=pltpu.SMEM)
    hbm = pl.BlockSpec(memory_space=pltpu.HBM)
    block = jax.ShapeDtypeStruct((halves, sides, LANES), jnp.float32)
    flat = jax.ShapeDtypeStruct(flat_d.shape, jnp.float32)

    def hop(value, axis, size, bit):
        return lax.ppermute(value, axis, [(at, at ^ bit) for at in range(size)])

    bits_s, bits_c = bits_of(cols)[:-1], bits_of(rows)
    stages = len(bits_s)
    assert stages > 1 and stages >= len(bits_c) - 1
    far = 2 * stages
    spots, lists = pl.pallas_call(
        functools.partial(plan_kernel, rows, cols, owned),
        out_shape=[
            jax.ShapeDtypeStruct((owned, 3, tile_size, LANES), jnp.float32),
            jax.ShapeDtypeStruct(((far + 1) * (2 * slots + 1) + 1,), jnp.int32),
        ],
        in_specs=[smem, hbm, hbm],
        out_specs=[vmem, smem],
        scratch_shapes=[
            pltpu.SMEM(pairs.shape, jnp.int32),
            pltpu.VMEM(flat_c.shape, jnp.float32),
            pltpu.SMEM((far + 1,), jnp.int32),
            pltpu.SemaphoreType.DMA((2,)),
        ],
        compiler_params=pltpu.CompilerParams(vmem_limit_bytes=8 << 20),
        cost_estimate=pl.CostEstimate(flops=10**9, bytes_accessed=10**5, transcendentals=0),
        name="plan",
    )(tile_count, *[pltpu.with_memory_space_constraint(value, pltpu.HBM) for value in (pairs, flat_c)])

    def near(groups, stacks):
        return pl.pallas_call(
            functools.partial(near_kernel, owned, groups, far, slots),
            out_shape=block,
            in_specs=[smem] + [vmem] * (1 + len(stacks)),
            out_specs=vmem,
            compiler_params=pltpu.CompilerParams(vmem_limit_bytes=16 << 20),
            cost_estimate=pl.CostEstimate(flops=10**10, bytes_accessed=10**6, transcendentals=0),
            name="near",
        )(lists, spots, *stacks)

    moved = [hop(flat_d, "col", cols, bits_s[0]), hop(flat_c, "col", cols, bits_s[0])]
    held_c = flat_c
    moved_c = hop(held_c, "row", rows, bits_c[0])
    *moved, moved_c = lax.optimization_barrier((*moved, moved_c))
    stacks = [lax.optimization_barrier(jnp.concatenate([flat_d, flat_c] + moved, axis=0))]
    swapped, terms = [], []
    for at in range(stages):
        fresh = None
        if at < stages - 1:
            sent = stacks[0] if at == 0 else jnp.concatenate(stacks, axis=0)
            fresh = hop(sent, "col", cols, bits_s[at + 1])
        if at + 1 < len(bits_c):
            held_c = jnp.concatenate([held_c, moved_c], axis=0)
            moved_c = hop(held_c, "row", rows, bits_c[at + 1])
        swapped.append(hop(stacks[at], "col", cols, 1))
        term = near([0], [stacks[0]]) if at == 0 else near([stages + at - 1], [swapped[at - 1]])
        if fresh is None:
            term, swapped[at], moved_c = lax.optimization_barrier((term, swapped[at], moved_c))
        else:
            term, fresh, moved_c = lax.optimization_barrier((term, fresh, moved_c))
            stacks.append(fresh)
        terms.append(term)
    heights = sum(stack.shape[0] for stack in stacks + swapped)
    partials = pl.pallas_call(
        functools.partial(far_kernel, rows, owned, far, slots),
        out_shape=[block] * (rows - 1),
        in_specs=[smem] + [vmem] * (2 + far),
        out_specs=[vmem] * (rows - 1),
        scratch_shapes=[
            pltpu.VMEM((heights, LANES), jnp.float32),
            pltpu.VMEM(((rows - 1) * owned, 3, tile_size, LANES), jnp.float32),
            pltpu.VMEM(((rows - 1) * halves, sides, LANES), jnp.float32),
            pltpu.SMEM(((rows - 1) * owned,), jnp.int32),
        ],
        compiler_params=pltpu.CompilerParams(vmem_limit_bytes=36 << 20),
        cost_estimate=pl.CostEstimate(flops=10**10, bytes_accessed=10**6, transcendentals=0),
        name="far",
    )(lists, held_c, moved_c, *stacks, *swapped)
    *partials, spots = lax.optimization_barrier((*partials, spots))
    terms.append(near(list(range(1, stages)), stacks[1:]))
    *partials, spots, terms[-1] = lax.optimization_barrier((*partials, spots, terms[-1]))
    arrived = [hop(partials[mask - 1], "row", rows, mask) for mask in range(1, rows)]
    terms.append(near([far - 1], swapped[-1:]))
    *arrived, terms[-1] = lax.optimization_barrier((*arrived, terms[-1]))
    terms = terms + arrived
    applied, stats = pl.pallas_call(
        functools.partial(sums_kernel, len(terms)),
        out_shape=[block, jax.ShapeDtypeStruct((parts, LANES), jnp.float32)],
        in_specs=[vmem] * (3 + len(terms)),
        out_specs=[vmem] * 2,
        scratch_shapes=[pltpu.VMEM((LANES, LANES), jnp.float32)],
        compiler_params=pltpu.CompilerParams(vmem_limit_bytes=4 << 20),
        name="sums",
    )(flat_r, flat_d, noise_var.reshape(-1, LANES), *terms)
    stats = lax.all_to_all(stats, ("row", "col"), 0, 0, tiled=True)
    new_x, new_r, new_d = pl.pallas_call(
        step_kernel,
        out_shape=[flat] * 3,
        in_specs=[vmem] * 5,
        out_specs=[vmem] * 3,
        compiler_params=pltpu.CompilerParams(vmem_limit_bytes=4 << 20),
        name="step",
    )(stats, applied, flat_x, flat_r, flat_d)
    return tuple(new.reshape(direction.shape) for new in (new_x, new_r, new_d))


def solution(mesh):
    field = P(None, None, "row", "col", None)
    in_specs = (
        field,
        field,
        field,
        P(None, "row", "col", None),
        field,
        P(None, "row", "col", None),
        P("row", "col"),
    )
    return jax.shard_map(
        functools.partial(per_device, mesh.shape["row"], mesh.shape["col"]),
        mesh=mesh,
        in_specs=in_specs,
        out_specs=(field, field, field),
        check_vma=False,
    )
```

```python
import functools
import jax
import jax.numpy as jnp
from jax import lax
from jax.experimental import pallas as pl
from jax.experimental.pallas import tpu as pltpu
from jax.sharding import PartitionSpec as P

EPS = 1e-06
SCALED_KERNEL = 0.125 / 256.0
TINY = 1e-30
LANES = 128
SIDES = 8
GROUP = 8


def bits_of(size):
    found = []
    bit = size // 2
    while bit:
        found.append(bit)
        bit //= 2
    return found


def masks(size):
    found = [0]
    for bit in bits_of(size):
        found = found + [mask ^ bit for mask in found]
    return found


def spread_tile(spots, slot, turned, tile, stride):
    for axis in range(3):
        for half in range(2):
            lane = axis * stride + 2 * tile + half
            spots[slot, axis, pl.ds(LANES * half, LANES), :] = jnp.broadcast_to(
                turned[:, lane : lane + 1], (LANES, LANES)
            )


def spread_kernel(owned, coords_ref, spots_ref):
    turned = 4.0 * jnp.transpose(coords_ref[...])
    for tile in range(owned):
        spread_tile(spots_ref, tile, turned, tile, 2 * owned)


def plan_kernel(rows, cols, owned, count, pairs_hbm, lists, pairs, sem):
    copy = pltpu.make_async_copy(pairs_hbm, pairs, sem)
    copy.start()
    my_row = lax.axis_index("row")
    my_col = lax.axis_index("col")
    bits = bits_of(cols)[:-1]
    stages = len(bits)
    far = 2 * stages
    height = (SIDES + 3) * 2 * owned
    slots = pairs.shape[1]
    head = far + 2
    for at in range(far + 1):
        lists[at] = 0
    copy.wait()

    def sort_pair(slot, carry):
        row_tile = pairs[0, slot]
        col_tile = pairs[1, slot]
        source = lax.bitwise_xor(row_tile & (cols - 1), my_col)
        target = lax.bitwise_xor(col_tile & (rows - 1), my_row)
        core = source & 1
        goal = lax.shift_right_logical(col_tile, rows.bit_length() - 1)
        place = lax.shift_right_logical(source, bits[0].bit_length() - 1) & 1
        near_place = place
        group = core * stages
        for at in range(1, stages):
            here = lax.shift_right_logical(source, bits[at].bit_length() - 1) & 1
            group = jnp.where(here == 1, at + core * stages, group)
            near_place = jnp.where(here == 1, place, near_place)
            place = place + here * 2**at
        is_near = target == 0
        group = jnp.where(is_near, group, far)
        place = jnp.where(is_near, near_place, place + core * (cols // 2))
        goal = jnp.where(is_near, goal, goal + (target - 1) * owned)
        found = lists[group]
        entry = head + 2 * (group * slots + found)
        lists[entry] = place * height + 2 * lax.shift_right_logical(row_tile, cols.bit_length() - 1)
        lists[entry + 1] = goal
        lists[group] = found + 1
        return carry

    lax.fori_loop(0, count[0, 0], sort_pair, jnp.int32(0))
    lists[far + 1] = (4 * lists[far] > lists[stages]).astype(jnp.int32)


def add_pairs(owned, found, base, lists, stack, spots, totals):
    stride = 2 * owned
    held = SIDES * stride

    def add_pair(slot):
        top = lists[base + 2 * slot]
        goal = lists[base + 2 * slot + 1]
        lhs_parts, near = [], []
        for side in range(2):
            values = stack[pl.ds(top + side, SIDES, stride=stride), :]
            lead = values.astype(jnp.bfloat16)
            rest = (values - lead.astype(jnp.float32)).astype(jnp.bfloat16)
            lhs_parts.append(jnp.concatenate([lead, rest], axis=0))
            near.append(
                [
                    jnp.broadcast_to(4.0 * stack[pl.ds(top + held + axis * stride + side, 1), :], (16, LANES))
                    for axis in range(3)
                ]
            )
        high_parts, low_parts = [], []
        for step in range(2 * LANES // 16):
            grid = [spots[goal, axis, pl.ds(16 * step, 16), :] for axis in range(3)]
            halves_high, halves_low = [], []
            for side in range(2):
                dx = grid[0] - near[side][0]
                dy = grid[1] - near[side][1]
                dz = grid[2] - near[side][2]
                square = dx * dx + dy * dy + dz * dz
                distance = square * lax.rsqrt(jnp.maximum(square, TINY))
                left = jnp.maximum(4.0 - distance, 0.0)
                left = left * left
                weight = left * left * (distance + 1.0)
                high = weight.astype(jnp.bfloat16)
                halves_high.append(high)
                halves_low.append((weight - high.astype(jnp.float32)).astype(jnp.bfloat16))
            high_parts.append(jnp.concatenate(halves_high, axis=1))
            low_parts.append(jnp.concatenate(halves_low, axis=1))
        lhs = jnp.concatenate(lhs_parts, axis=1)
        dims = (((1,), (1,)), ((), ()))
        product = lax.dot_general(
            lhs, jnp.concatenate(high_parts, axis=0), dims, preferred_element_type=jnp.float32
        ) + lax.dot_general(
            lhs, jnp.concatenate(low_parts, axis=0), dims, preferred_element_type=jnp.float32
        )
        summed = product[:SIDES] + product[SIDES:]
        for half in range(2):
            totals[2 * goal + half] += summed[:, LANES * half : LANES * half + LANES]

    whole = lax.div(found, GROUP)

    def add_group(step, carry):
        for part in range(GROUP):
            add_pair(GROUP * step + part)
        return carry

    def add_one(slot, carry):
        add_pair(slot)
        return carry

    lax.fori_loop(0, whole, add_group, jnp.int32(0))
    lax.fori_loop(GROUP * whole, found, add_one, jnp.int32(0))


def near_kernel(owned, groups, far, slots, lists, spots, *refs):
    totals = refs[-1]
    totals[...] = jnp.zeros_like(totals)
    for (group, flag), stack in zip(groups, refs):
        base = far + 2 + 2 * group * slots
        found = lists[group]
        if flag is not None:
            found = jnp.where(lists[far + 1] == flag, found, 0)
        add_pairs(owned, found, base, lists, stack, spots, totals)


def far_kernel(rows, owned, far, slots, lists, *refs):
    points = refs[:2]
    stacks = refs[2 : 2 + far]
    outs = refs[2 + far : 1 + far + rows]
    slab, spots, totals, wanted = refs[1 + far + rows :]
    stride = 2 * owned
    spread = 3 * stride
    found = lists[far]
    base = far + 2 + 2 * far * slots

    @pl.when(found == 0)
    def _():
        for out in outs:
            out[...] = jnp.zeros_like(out)

    @pl.when(found > 0)
    def _():
        for tile in range((rows - 1) * owned):
            wanted[tile] = 0

        def want(slot, carry):
            wanted[lists[base + 2 * slot + 1]] = 1
            return carry

        lax.fori_loop(0, found, want, jnp.int32(0))
        totals[...] = jnp.zeros_like(totals)
        top = 0
        for stack in stacks:
            slab[pl.ds(top, stack.shape[0]), :] = stack[...]
            top += stack.shape[0]
        for place, mask in enumerate(masks(rows)):
            if mask:
                top = (place % (rows // 2)) * spread
                turned = 4.0 * jnp.transpose(points[place // (rows // 2)][pl.ds(top, spread), :])
                for tile in range(owned):
                    slot = (mask - 1) * owned + tile

                    @pl.when(wanted[slot] == 1)
                    def _():
                        spread_tile(spots, slot, turned, tile, stride)

        add_pairs(owned, found, base, lists, slab, spots, totals)
        for at in range(rows - 1):
            outs[at][...] = totals[pl.ds(at * stride, stride)]


def sums_kernel(terms, residual_ref, direction_ref, noise_ref, *refs):
    partials = refs[:terms]
    applied_ref, stats_ref, stack = refs[terms:]
    halves = noise_ref.shape[0]
    zero = jnp.zeros((SIDES, LANES), jnp.float32)
    now, bend, cross, size = zero, zero, zero, zero
    for part in range(halves):
        total = partials[0][part]
        for other in partials[1:]:
            total = total + other[part]
        residual = residual_ref[pl.ds(part, SIDES, stride=halves), :]
        direction = direction_ref[pl.ds(part, SIDES, stride=halves), :]
        applied = noise_ref[part : part + 1, :] * direction + SCALED_KERNEL * total
        applied_ref[part] = applied
        now = now + residual * residual
        bend = bend + direction * applied
        cross = cross + residual * applied
        size = size + applied * applied
    stack[...] = jnp.zeros_like(stack)
    for slot, value in enumerate((now, bend, cross, size)):
        stack[SIDES * slot : SIDES * slot + SIDES, :] = value
    stats_ref[...] = lax.dot_general(
        jnp.ones((stats_ref.shape[0], LANES), jnp.float32),
        stack[...],
        (((1,), (1,)), ((), ())),
        precision=lax.Precision.HIGHEST,
        preferred_element_type=jnp.float32,
    )


def step_kernel(
    stats_ref, applied_ref, solution_ref, residual_ref, direction_ref, new_x, new_r, new_d
):
    halves = applied_ref.shape[0]
    summed = jnp.sum(stats_ref[...], axis=0, keepdims=True)
    summed = jnp.broadcast_to(summed, (SIDES, LANES))
    lane = lax.broadcasted_iota(jnp.int32, (SIDES, LANES), 1)
    line = lax.broadcasted_iota(jnp.int32, (SIDES, LANES), 0)

    def pick(slot):
        return jnp.sum(
            jnp.where(lane == line + SIDES * slot, summed, 0.0), axis=1, keepdims=True
        )

    now, bend, cross, size = pick(0), pick(1), pick(2), pick(3)
    step = now / bend
    after = jnp.maximum(now - 2.0 * step * cross + step * step * size, 0.0)
    beta = jnp.broadcast_to(after / (now + EPS), (SIDES, LANES))
    step = jnp.broadcast_to(step, (SIDES, LANES))
    for part in range(halves):
        place = pl.ds(part, SIDES, stride=halves)
        direction = direction_ref[place, :]
        new_x[place, :] = solution_ref[place, :] + step * direction
        residual = residual_ref[place, :] - step * applied_ref[part]
        new_r[place, :] = residual
        new_d[place, :] = residual + beta * direction


def per_device(rows, cols, solution, residual, direction, noise_var, coords, tile_pairs, tile_count):
    sides, owned, _, _, tile_size = direction.shape
    assert sides == SIDES and tile_size == 2 * LANES
    assert rows & (rows - 1) == 0 and cols & (cols - 1) == 0 and cols >= rows > 1 and cols > 2
    parts = rows * cols
    halves = 2 * owned
    flat_x = solution.reshape(-1, LANES)
    flat_r = residual.reshape(-1, LANES)
    flat_d = direction.reshape(-1, LANES)
    flat_c = coords.reshape(-1, LANES)
    pairs = tile_pairs.reshape(2, -1)
    slots = pairs.shape[1]
    vmem = pl.BlockSpec(memory_space=pltpu.VMEM)
    smem = pl.BlockSpec(memory_space=pltpu.SMEM)
    hbm = pl.BlockSpec(memory_space=pltpu.HBM)
    block = jax.ShapeDtypeStruct((halves, sides, LANES), jnp.float32)
    flat = jax.ShapeDtypeStruct(flat_d.shape, jnp.float32)

    def hop(value, axis, size, bit):
        return lax.ppermute(value, axis, [(at, at ^ bit) for at in range(size)])

    bits_s, bits_c = bits_of(cols)[:-1], bits_of(rows)
    stages = len(bits_s)
    assert stages > 1 and stages >= len(bits_c) - 1
    far = 2 * stages
    lists = pl.pallas_call(
        functools.partial(plan_kernel, rows, cols, owned),
        out_shape=jax.ShapeDtypeStruct((far + 2 + 2 * (far + 1) * slots,), jnp.int32),
        in_specs=[smem, hbm],
        out_specs=smem,
        scratch_shapes=[pltpu.SMEM(pairs.shape, jnp.int32), pltpu.SemaphoreType.DMA(())],
        compiler_params=pltpu.CompilerParams(vmem_limit_bytes=8 << 20),
        cost_estimate=pl.CostEstimate(flops=10**9, bytes_accessed=10**5, transcendentals=0),
        name="plan",
    )(tile_count, pltpu.with_memory_space_constraint(pairs, pltpu.HBM))

    def near(groups, stacks):
        return pl.pallas_call(
            functools.partial(near_kernel, owned, groups, far, slots),
            out_shape=block,
            in_specs=[smem] + [vmem] * (1 + len(stacks)),
            out_specs=vmem,
            compiler_params=pltpu.CompilerParams(vmem_limit_bytes=16 << 20),
            cost_estimate=pl.CostEstimate(flops=10**10, bytes_accessed=10**6, transcendentals=0),
            name="near",
        )(lists, spots, *stacks)

    moved = [hop(flat_d, "col", cols, bits_s[0]), hop(flat_c, "col", cols, bits_s[0])]
    held_c = flat_c
    moved_c = hop(held_c, "row", rows, bits_c[0])
    *moved, moved_c, lists = lax.optimization_barrier((*moved, moved_c, lists))
    stack, own_c = lax.optimization_barrier(
        (jnp.concatenate([flat_d, flat_c] + moved, axis=0), flat_c)
    )
    stacks = [stack]
    spots = pl.pallas_call(
        functools.partial(spread_kernel, owned),
        out_shape=jax.ShapeDtypeStruct((owned, 3, tile_size, LANES), jnp.float32),
        in_specs=[vmem],
        out_specs=vmem,
        compiler_params=pltpu.CompilerParams(vmem_limit_bytes=8 << 20),
        cost_estimate=pl.CostEstimate(flops=10**9, bytes_accessed=10**5, transcendentals=0),
        name="spread",
    )(own_c)
    swapped, terms = [], []
    for at in range(stages):
        fresh = None
        if at < stages - 1:
            sent = stacks[0] if at == 0 else jnp.concatenate(stacks, axis=0)
            fresh = hop(sent, "col", cols, bits_s[at + 1])
        if at + 1 < len(bits_c):
            held_c = jnp.concatenate([held_c, moved_c], axis=0)
            moved_c = hop(held_c, "row", rows, bits_c[at + 1])
        swapped.append(hop(stacks[at], "col", cols, 1))
        if at == 0:
            term = near([(0, None)], stacks)
        else:
            term = near([(stages + at - 1, 0)], [swapped[at - 1]])
        if fresh is None:
            term, swapped[at], moved_c = lax.optimization_barrier((term, swapped[at], moved_c))
        else:
            term, fresh, moved_c = lax.optimization_barrier((term, fresh, moved_c))
            stacks.append(fresh)
        terms.append(term)
    heights = sum(stack.shape[0] for stack in stacks + swapped)
    partials = pl.pallas_call(
        functools.partial(far_kernel, rows, owned, far, slots),
        out_shape=[block] * (rows - 1),
        in_specs=[smem] + [vmem] * (2 + far),
        out_specs=[vmem] * (rows - 1),
        scratch_shapes=[
            pltpu.VMEM((heights, LANES), jnp.float32),
            pltpu.VMEM(((rows - 1) * owned, 3, tile_size, LANES), jnp.float32),
            pltpu.VMEM(((rows - 1) * halves, sides, LANES), jnp.float32),
            pltpu.SMEM(((rows - 1) * owned,), jnp.int32),
        ],
        compiler_params=pltpu.CompilerParams(vmem_limit_bytes=36 << 20),
        cost_estimate=pl.CostEstimate(flops=10**10, bytes_accessed=10**6, transcendentals=0),
        name="far",
    )(lists, held_c, moved_c, *stacks, *swapped)
    late = [(at, None) for at in range(1, stages)] + [(far - 1, None)]
    late = late + [(stages + at, 1) for at in range(stages - 1)]
    *partials, spots = lax.optimization_barrier((*partials, spots))
    arrived = [hop(partials[mask - 1], "row", rows, mask) for mask in range(1, rows)]
    terms.append(near(late, stacks[1:] + swapped[-1:] + swapped[:-1]))
    *arrived, terms[-1] = lax.optimization_barrier((*arrived, terms[-1]))
    terms = terms + arrived
    applied, stats = pl.pallas_call(
        functools.partial(sums_kernel, len(terms)),
        out_shape=[block, jax.ShapeDtypeStruct((parts, LANES), jnp.float32)],
        in_specs=[vmem] * (3 + len(terms)),
        out_specs=[vmem] * 2,
        scratch_shapes=[pltpu.VMEM((LANES, LANES), jnp.float32)],
        compiler_params=pltpu.CompilerParams(vmem_limit_bytes=4 << 20),
        name="sums",
    )(flat_r, flat_d, noise_var.reshape(-1, LANES), *terms)
    stats = lax.all_to_all(stats, ("row", "col"), 0, 0, tiled=True)
    new_x, new_r, new_d = pl.pallas_call(
        step_kernel,
        out_shape=[flat] * 3,
        in_specs=[vmem] * 5,
        out_specs=[vmem] * 3,
        compiler_params=pltpu.CompilerParams(vmem_limit_bytes=4 << 20),
        name="step",
    )(stats, applied, flat_x, flat_r, flat_d)
    return tuple(new.reshape(direction.shape) for new in (new_x, new_r, new_d))


def solution(mesh):
    field = P(None, None, "row", "col", None)
    in_specs = (
        field,
        field,
        field,
        P(None, "row", "col", None),
        field,
        P(None, "row", "col", None),
        P("row", "col"),
    )
    return jax.shard_map(
        functools.partial(per_device, mesh.shape["row"], mesh.shape["col"]),
        mesh=mesh,
        in_specs=in_specs,
        out_specs=(field, field, field),
        check_vma=False,
    )
```

```python
import functools
import jax
import jax.numpy as jnp
from jax import lax
from jax.experimental import pallas as pl
from jax.experimental.pallas import tpu as pltpu
from jax.sharding import PartitionSpec as P

EPS = 1e-06
SCALED_KERNEL = 0.125 / 256.0
TINY = 1e-30
LANES = 128
SIDES = 8
GROUP = 8


def bits_of(size):
    found = []
    bit = size // 2
    while bit:
        found.append(bit)
        bit //= 2
    return found


def masks(size):
    found = [0]
    for bit in bits_of(size):
        found = found + [mask ^ bit for mask in found]
    return found


def spread_tile(spots, slot, turned, tile, stride):
    for axis in range(3):
        for half in range(2):
            lane = axis * stride + 2 * tile + half
            spots[slot, axis, pl.ds(LANES * half, LANES), :] = jnp.broadcast_to(
                turned[:, lane : lane + 1], (LANES, LANES)
            )


def spread_kernel(owned, coords_ref, spots_ref):
    turned = 4.0 * jnp.transpose(coords_ref[...])
    for tile in range(owned):
        spread_tile(spots_ref, tile, turned, tile, 2 * owned)


def plan_kernel(rows, cols, owned, count, pairs_hbm, lists, pairs, tally, sem):
    copy = pltpu.make_async_copy(pairs_hbm, pairs, sem)
    copy.start()
    my_row = lax.axis_index("row")
    my_col = lax.axis_index("col")
    bits = bits_of(cols)[:-1]
    stages = len(bits)
    far = 2 * stages
    height = (SIDES + 3) * 2 * owned
    slots = pairs.shape[1]
    head = far + 2
    for at in range(far + 1):
        tally[at] = 0
    live = count[0, 0]
    copy.wait()

    def sort_four(step, carry):
        sorted_pairs = []
        for part in range(4):
            slot = 4 * step + part
            row_tile = pairs[0, slot]
            col_tile = pairs[1, slot]
            source = lax.bitwise_xor(row_tile & (cols - 1), my_col)
            target = lax.bitwise_xor(col_tile & (rows - 1), my_row)
            core = source & 1
            goal = lax.shift_right_logical(col_tile, rows.bit_length() - 1)
            place = lax.shift_right_logical(source, bits[0].bit_length() - 1) & 1
            near_place = place
            group = core * stages
            for at in range(1, stages):
                here = lax.shift_right_logical(source, bits[at].bit_length() - 1) & 1
                group = jnp.where(here == 1, at + core * stages, group)
                near_place = jnp.where(here == 1, place, near_place)
                place = place + here * 2**at
            is_near = target == 0
            group = jnp.where(is_near, group, far)
            place = jnp.where(is_near, near_place, place + core * (cols // 2))
            goal = jnp.where(is_near, goal, goal + (target - 1) * owned)
            top = place * height + 2 * lax.shift_right_logical(row_tile, cols.bit_length() - 1)
            sorted_pairs.append((group, top * 256 + goal, (slot < live).astype(jnp.int32)))
        for group, entry, kept in sorted_pairs:
            found = tally[group]
            lists[head + group * slots + found] = entry
            tally[group] = found + kept
        return carry

    lax.fori_loop(0, lax.shift_right_logical(live + 3, 2), sort_four, jnp.int32(0))
    for at in range(far + 1):
        lists[at] = tally[at]
    lists[far + 1] = (4 * tally[far] > tally[stages]).astype(jnp.int32)


def add_pairs(owned, found, base, lists, stack, spots, totals):
    stride = 2 * owned
    held = SIDES * stride

    def add_pair(slot):
        entry = lists[base + slot]
        top = lax.shift_right_logical(entry, 8)
        goal = entry & 255
        lhs_parts, near = [], []
        for side in range(2):
            values = stack[pl.ds(top + side, SIDES, stride=stride), :]
            lead = values.astype(jnp.bfloat16)
            rest = (values - lead.astype(jnp.float32)).astype(jnp.bfloat16)
            lhs_parts.append(jnp.concatenate([lead, rest], axis=0))
            near.append(
                [
                    jnp.broadcast_to(4.0 * stack[pl.ds(top + held + axis * stride + side, 1), :], (16, LANES))
                    for axis in range(3)
                ]
            )
        high_parts, low_parts = [], []
        for step in range(2 * LANES // 16):
            grid = [spots[goal, axis, pl.ds(16 * step, 16), :] for axis in range(3)]
            halves_high, halves_low = [], []
            for side in range(2):
                dx = grid[0] - near[side][0]
                dy = grid[1] - near[side][1]
                dz = grid[2] - near[side][2]
                square = dx * dx + dy * dy + dz * dz
                distance = square * lax.rsqrt(jnp.maximum(square, TINY))
                left = jnp.maximum(4.0 - distance, 0.0)
                left = left * left
                weight = left * left * (distance + 1.0)
                high = weight.astype(jnp.bfloat16)
                halves_high.append(high)
                halves_low.append((weight - high.astype(jnp.float32)).astype(jnp.bfloat16))
            high_parts.append(jnp.concatenate(halves_high, axis=1))
            low_parts.append(jnp.concatenate(halves_low, axis=1))
        lhs = jnp.concatenate(lhs_parts, axis=1)
        dims = (((1,), (1,)), ((), ()))
        product = lax.dot_general(
            lhs, jnp.concatenate(high_parts, axis=0), dims, preferred_element_type=jnp.float32
        ) + lax.dot_general(
            lhs, jnp.concatenate(low_parts, axis=0), dims, preferred_element_type=jnp.float32
        )
        summed = product[:SIDES] + product[SIDES:]
        for half in range(2):
            totals[2 * goal + half] += summed[:, LANES * half : LANES * half + LANES]

    whole = lax.div(found, GROUP)

    def add_group(step, carry):
        for part in range(GROUP):
            add_pair(GROUP * step + part)
        return carry

    def add_one(slot, carry):
        add_pair(slot)
        return carry

    lax.fori_loop(0, whole, add_group, jnp.int32(0))
    lax.fori_loop(GROUP * whole, found, add_one, jnp.int32(0))


def near_kernel(owned, groups, far, slots, lists, spots, *refs):
    totals = refs[-1]
    totals[...] = jnp.zeros_like(totals)
    for (group, flag), stack in zip(groups, refs):
        base = far + 2 + group * slots
        found = lists[group]
        if flag is not None:
            found = jnp.where(lists[far + 1] == flag, found, 0)
        add_pairs(owned, found, base, lists, stack, spots, totals)


def far_kernel(rows, owned, far, slots, lists, *refs):
    points = refs[:2]
    stacks = refs[2 : 2 + far]
    outs = refs[2 + far : 1 + far + rows]
    slab, spots, totals, wanted = refs[1 + far + rows :]
    stride = 2 * owned
    spread = 3 * stride
    found = lists[far]
    base = far + 2 + far * slots

    @pl.when(found == 0)
    def _():
        for out in outs:
            out[...] = jnp.zeros_like(out)

    @pl.when(found > 0)
    def _():
        for tile in range((rows - 1) * owned):
            wanted[tile] = 0

        def want(slot, carry):
            wanted[lists[base + slot] & 255] = 1
            return carry

        lax.fori_loop(0, found, want, jnp.int32(0))
        totals[...] = jnp.zeros_like(totals)
        top = 0
        for stack in stacks:
            slab[pl.ds(top, stack.shape[0]), :] = stack[...]
            top += stack.shape[0]
        for place, mask in enumerate(masks(rows)):
            if mask:
                top = (place % (rows // 2)) * spread
                turned = 4.0 * jnp.transpose(points[place // (rows // 2)][pl.ds(top, spread), :])
                for tile in range(owned):
                    slot = (mask - 1) * owned + tile

                    @pl.when(wanted[slot] == 1)
                    def _():
                        spread_tile(spots, slot, turned, tile, stride)

        add_pairs(owned, found, base, lists, slab, spots, totals)
        for at in range(rows - 1):
            outs[at][...] = totals[pl.ds(at * stride, stride)]


def sums_kernel(terms, residual_ref, direction_ref, noise_ref, *refs):
    partials = refs[:terms]
    applied_ref, stats_ref, stack = refs[terms:]
    halves = noise_ref.shape[0]
    zero = jnp.zeros((SIDES, LANES), jnp.float32)
    now, bend, cross, size = zero, zero, zero, zero
    for part in range(halves):
        total = partials[0][part]
        for other in partials[1:]:
            total = total + other[part]
        residual = residual_ref[pl.ds(part, SIDES, stride=halves), :]
        direction = direction_ref[pl.ds(part, SIDES, stride=halves), :]
        applied = noise_ref[part : part + 1, :] * direction + SCALED_KERNEL * total
        applied_ref[part] = applied
        now = now + residual * residual
        bend = bend + direction * applied
        cross = cross + residual * applied
        size = size + applied * applied
    stack[...] = jnp.zeros_like(stack)
    for slot, value in enumerate((now, bend, cross, size)):
        stack[SIDES * slot : SIDES * slot + SIDES, :] = value
    stats_ref[...] = lax.dot_general(
        jnp.ones((stats_ref.shape[0], LANES), jnp.float32),
        stack[...],
        (((1,), (1,)), ((), ())),
        precision=lax.Precision.HIGHEST,
        preferred_element_type=jnp.float32,
    )


def step_kernel(
    stats_ref, applied_ref, solution_ref, residual_ref, direction_ref, new_x, new_r, new_d
):
    halves = applied_ref.shape[0]
    summed = jnp.sum(stats_ref[...], axis=0, keepdims=True)
    summed = jnp.broadcast_to(summed, (SIDES, LANES))
    lane = lax.broadcasted_iota(jnp.int32, (SIDES, LANES), 1)
    line = lax.broadcasted_iota(jnp.int32, (SIDES, LANES), 0)

    def pick(slot):
        return jnp.sum(
            jnp.where(lane == line + SIDES * slot, summed, 0.0), axis=1, keepdims=True
        )

    now, bend, cross, size = pick(0), pick(1), pick(2), pick(3)
    step = now / bend
    after = jnp.maximum(now - 2.0 * step * cross + step * step * size, 0.0)
    beta = jnp.broadcast_to(after / (now + EPS), (SIDES, LANES))
    step = jnp.broadcast_to(step, (SIDES, LANES))
    for part in range(halves):
        place = pl.ds(part, SIDES, stride=halves)
        direction = direction_ref[place, :]
        new_x[place, :] = solution_ref[place, :] + step * direction
        residual = residual_ref[place, :] - step * applied_ref[part]
        new_r[place, :] = residual
        new_d[place, :] = residual + beta * direction


def per_device(rows, cols, solution, residual, direction, noise_var, coords, tile_pairs, tile_count):
    sides, owned, _, _, tile_size = direction.shape
    assert sides == SIDES and tile_size == 2 * LANES
    assert tile_pairs.shape[-1] % 4 == 0 and (rows - 1) * owned <= 256
    assert rows & (rows - 1) == 0 and cols & (cols - 1) == 0 and cols >= rows > 1 and cols > 2
    parts = rows * cols
    halves = 2 * owned
    flat_x = solution.reshape(-1, LANES)
    flat_r = residual.reshape(-1, LANES)
    flat_d = direction.reshape(-1, LANES)
    flat_c = coords.reshape(-1, LANES)
    pairs = tile_pairs.reshape(2, -1)
    slots = pairs.shape[1]
    vmem = pl.BlockSpec(memory_space=pltpu.VMEM)
    smem = pl.BlockSpec(memory_space=pltpu.SMEM)
    hbm = pl.BlockSpec(memory_space=pltpu.HBM)
    block = jax.ShapeDtypeStruct((halves, sides, LANES), jnp.float32)
    flat = jax.ShapeDtypeStruct(flat_d.shape, jnp.float32)

    def hop(value, axis, size, bit):
        return lax.ppermute(value, axis, [(at, at ^ bit) for at in range(size)])

    bits_s, bits_c = bits_of(cols)[:-1], bits_of(rows)
    stages = len(bits_s)
    assert stages > 1 and stages >= len(bits_c) - 1
    far = 2 * stages
    lists = pl.pallas_call(
        functools.partial(plan_kernel, rows, cols, owned),
        out_shape=jax.ShapeDtypeStruct((far + 2 + (far + 1) * slots,), jnp.int32),
        in_specs=[smem, hbm],
        out_specs=smem,
        scratch_shapes=[
            pltpu.SMEM(pairs.shape, jnp.int32),
            pltpu.SMEM((far + 1,), jnp.int32),
            pltpu.SemaphoreType.DMA(()),
        ],
        compiler_params=pltpu.CompilerParams(vmem_limit_bytes=8 << 20),
        cost_estimate=pl.CostEstimate(flops=10**9, bytes_accessed=10**5, transcendentals=0),
        name="plan",
    )(tile_count, pltpu.with_memory_space_constraint(pairs, pltpu.HBM))

    def near(groups, stacks):
        return pl.pallas_call(
            functools.partial(near_kernel, owned, groups, far, slots),
            out_shape=block,
            in_specs=[smem] + [vmem] * (1 + len(stacks)),
            out_specs=vmem,
            compiler_params=pltpu.CompilerParams(vmem_limit_bytes=16 << 20),
            cost_estimate=pl.CostEstimate(flops=10**10, bytes_accessed=10**6, transcendentals=0),
            name="near",
        )(lists, spots, *stacks)

    moved = [hop(flat_d, "col", cols, bits_s[0]), hop(flat_c, "col", cols, bits_s[0])]
    held_c = flat_c
    moved_c = hop(held_c, "row", rows, bits_c[0])
    *moved, moved_c, lists = lax.optimization_barrier((*moved, moved_c, lists))
    stack, own_c = lax.optimization_barrier(
        (jnp.concatenate([flat_d, flat_c] + moved, axis=0), flat_c)
    )
    stacks = [stack]
    spots = pl.pallas_call(
        functools.partial(spread_kernel, owned),
        out_shape=jax.ShapeDtypeStruct((owned, 3, tile_size, LANES), jnp.float32),
        in_specs=[vmem],
        out_specs=vmem,
        compiler_params=pltpu.CompilerParams(vmem_limit_bytes=8 << 20),
        cost_estimate=pl.CostEstimate(flops=10**9, bytes_accessed=10**5, transcendentals=0),
        name="spread",
    )(own_c)
    swapped, terms = [], []
    for at in range(stages):
        fresh = None
        if at < stages - 1:
            sent = stacks[0] if at == 0 else jnp.concatenate(stacks, axis=0)
            fresh = hop(sent, "col", cols, bits_s[at + 1])
        if at + 1 < len(bits_c):
            held_c = jnp.concatenate([held_c, moved_c], axis=0)
            moved_c = hop(held_c, "row", rows, bits_c[at + 1])
        swapped.append(hop(stacks[at], "col", cols, 1))
        if at == 0:
            term = near([(0, None)], stacks)
        else:
            term = near([(stages + at - 1, 0)], [swapped[at - 1]])
        if fresh is None:
            term, swapped[at], moved_c = lax.optimization_barrier((term, swapped[at], moved_c))
        else:
            term, fresh, moved_c = lax.optimization_barrier((term, fresh, moved_c))
            stacks.append(fresh)
        terms.append(term)
    heights = sum(stack.shape[0] for stack in stacks + swapped)
    partials = pl.pallas_call(
        functools.partial(far_kernel, rows, owned, far, slots),
        out_shape=[block] * (rows - 1),
        in_specs=[smem] + [vmem] * (2 + far),
        out_specs=[vmem] * (rows - 1),
        scratch_shapes=[
            pltpu.VMEM((heights, LANES), jnp.float32),
            pltpu.VMEM(((rows - 1) * owned, 3, tile_size, LANES), jnp.float32),
            pltpu.VMEM(((rows - 1) * halves, sides, LANES), jnp.float32),
            pltpu.SMEM(((rows - 1) * owned,), jnp.int32),
        ],
        compiler_params=pltpu.CompilerParams(vmem_limit_bytes=36 << 20),
        cost_estimate=pl.CostEstimate(flops=10**10, bytes_accessed=10**6, transcendentals=0),
        name="far",
    )(lists, held_c, moved_c, *stacks, *swapped)
    *partials, spots = lax.optimization_barrier((*partials, spots))
    half = rows // 2
    arrived = [hop(partials[half - 1], "row", rows, half)]
    terms.append(near([(at, None) for at in range(1, stages)], stacks[1:]))
    *partials, spots, terms[-1], arrived[0] = lax.optimization_barrier(
        (*partials, spots, terms[-1], arrived[0])
    )
    for mask in range(rows - 1, 0, -1):
        if mask != half:
            arrived.append(hop(partials[mask - 1], "row", rows, mask))
    late = [(far - 1, None)] + [(stages + at, 1) for at in range(stages - 1)]
    terms.append(near(late, swapped[-1:] + swapped[:-1]))
    *arrived, terms[-1] = lax.optimization_barrier((*arrived, terms[-1]))
    terms = terms + arrived
    applied, stats = pl.pallas_call(
        functools.partial(sums_kernel, len(terms)),
        out_shape=[block, jax.ShapeDtypeStruct((parts, LANES), jnp.float32)],
        in_specs=[vmem] * (3 + len(terms)),
        out_specs=[vmem] * 2,
        scratch_shapes=[pltpu.VMEM((LANES, LANES), jnp.float32)],
        compiler_params=pltpu.CompilerParams(vmem_limit_bytes=4 << 20),
        name="sums",
    )(flat_r, flat_d, noise_var.reshape(-1, LANES), *terms)
    stats = lax.all_to_all(stats, ("row", "col"), 0, 0, tiled=True)
    new_x, new_r, new_d = pl.pallas_call(
        step_kernel,
        out_shape=[flat] * 3,
        in_specs=[vmem] * 5,
        out_specs=[vmem] * 3,
        compiler_params=pltpu.CompilerParams(vmem_limit_bytes=4 << 20),
        name="step",
    )(stats, applied, flat_x, flat_r, flat_d)
    return tuple(new.reshape(direction.shape) for new in (new_x, new_r, new_d))


def solution(mesh):
    field = P(None, None, "row", "col", None)
    in_specs = (
        field,
        field,
        field,
        P(None, "row", "col", None),
        field,
        P(None, "row", "col", None),
        P("row", "col"),
    )
    return jax.shard_map(
        functools.partial(per_device, mesh.shape["row"], mesh.shape["col"]),
        mesh=mesh,
        in_specs=in_specs,
        out_specs=(field, field, field),
        check_vma=False,
    )
```

```python
import functools
import jax
import jax.numpy as jnp
from jax import lax
from jax.experimental import pallas as pl
from jax.experimental.pallas import tpu as pltpu
from jax.sharding import PartitionSpec as P

EPS = 1e-06
SCALED_KERNEL = 0.125 / 256.0
TINY = 1e-30
LANES = 128
SIDES = 8
GROUP = 8


def bits_of(size):
    found = []
    bit = size // 2
    while bit:
        found.append(bit)
        bit //= 2
    return found


def masks(size):
    found = [0]
    for bit in bits_of(size):
        found = found + [mask ^ bit for mask in found]
    return found


def spread_tile(spots, slot, turned, tile, stride):
    for axis in range(3):
        for half in range(2):
            lane = axis * stride + 2 * tile + half
            spots[slot, axis, pl.ds(LANES * half, LANES), :] = jnp.broadcast_to(
                turned[:, lane : lane + 1], (LANES, LANES)
            )


def plan_kernel(rows, cols, owned, count, pairs_hbm, lists, pairs, tally, sem):
    copy = pltpu.make_async_copy(pairs_hbm, pairs, sem)
    copy.start()
    my_row = lax.axis_index("row")
    my_col = lax.axis_index("col")
    bits = bits_of(cols)[:-1]
    stages = len(bits)
    far = 2 * stages
    height = (SIDES + 3) * 2 * owned
    slots = pairs.shape[1]
    head = far + 2
    for at in range(far + 1):
        tally[at] = 0
    live = count[0, 0]
    copy.wait()

    def sort_four(step, carry):
        sorted_pairs = []
        for part in range(4):
            slot = 4 * step + part
            row_tile = pairs[0, slot]
            col_tile = pairs[1, slot]
            source = lax.bitwise_xor(row_tile & (cols - 1), my_col)
            target = lax.bitwise_xor(col_tile & (rows - 1), my_row)
            core = source & 1
            goal = lax.shift_right_logical(col_tile, rows.bit_length() - 1)
            place = lax.shift_right_logical(source, bits[0].bit_length() - 1) & 1
            near_place = place
            group = core * stages
            for at in range(1, stages):
                here = lax.shift_right_logical(source, bits[at].bit_length() - 1) & 1
                group = jnp.where(here == 1, at + core * stages, group)
                near_place = jnp.where(here == 1, place, near_place)
                place = place + here * 2**at
            is_near = target == 0
            group = jnp.where(is_near, group, far)
            place = jnp.where(is_near, near_place, place + core * (cols // 2))
            goal = jnp.where(is_near, goal, goal + (target - 1) * owned)
            top = place * height + 2 * lax.shift_right_logical(row_tile, cols.bit_length() - 1)
            sorted_pairs.append((group, top * 256 + goal, (slot < live).astype(jnp.int32)))
        for group, entry, kept in sorted_pairs:
            found = tally[group]
            lists[head + group * slots + found] = entry
            tally[group] = found + kept
        return carry

    lax.fori_loop(0, lax.shift_right_logical(live + 3, 2), sort_four, jnp.int32(0))
    for at in range(far + 1):
        lists[at] = tally[at]
    lists[far + 1] = (4 * tally[far] > tally[stages]).astype(jnp.int32)


def add_pairs(owned, found, base, lists, stack, spots, totals):
    stride = 2 * owned
    held = SIDES * stride

    def add_pair(slot):
        entry = lists[base + slot]
        top = lax.shift_right_logical(entry, 8)
        goal = entry & 255
        lhs_parts, near = [], []
        for side in range(2):
            values = stack[pl.ds(top + side, SIDES, stride=stride), :]
            lead = values.astype(jnp.bfloat16)
            rest = (values - lead.astype(jnp.float32)).astype(jnp.bfloat16)
            lhs_parts.append(jnp.concatenate([lead, rest], axis=0))
            near.append(
                [
                    jnp.broadcast_to(4.0 * stack[pl.ds(top + held + axis * stride + side, 1), :], (16, LANES))
                    for axis in range(3)
                ]
            )
        high_parts, low_parts = [], []
        for step in range(2 * LANES // 16):
            grid = [spots[goal, axis, pl.ds(16 * step, 16), :] for axis in range(3)]
            halves_high, halves_low = [], []
            for side in range(2):
                dx = grid[0] - near[side][0]
                dy = grid[1] - near[side][1]
                dz = grid[2] - near[side][2]
                square = dx * dx + dy * dy + dz * dz
                distance = square * lax.rsqrt(jnp.maximum(square, TINY))
                left = jnp.maximum(4.0 - distance, 0.0)
                left = left * left
                weight = left * left * (distance + 1.0)
                high = weight.astype(jnp.bfloat16)
                halves_high.append(high)
                halves_low.append((weight - high.astype(jnp.float32)).astype(jnp.bfloat16))
            high_parts.append(jnp.concatenate(halves_high, axis=1))
            low_parts.append(jnp.concatenate(halves_low, axis=1))
        lhs = jnp.concatenate(lhs_parts, axis=1)
        dims = (((1,), (1,)), ((), ()))
        product = lax.dot_general(
            lhs, jnp.concatenate(high_parts, axis=0), dims, preferred_element_type=jnp.float32
        ) + lax.dot_general(
            lhs, jnp.concatenate(low_parts, axis=0), dims, preferred_element_type=jnp.float32
        )
        summed = product[:SIDES] + product[SIDES:]
        for half in range(2):
            totals[2 * goal + half] += summed[:, LANES * half : LANES * half + LANES]

    whole = lax.div(found, GROUP)

    def add_group(step, carry):
        for part in range(GROUP):
            add_pair(GROUP * step + part)
        return carry

    def add_one(slot, carry):
        add_pair(slot)
        return carry

    lax.fori_loop(0, whole, add_group, jnp.int32(0))
    lax.fori_loop(GROUP * whole, found, add_one, jnp.int32(0))


def near_kernel(owned, groups, far, slots, lists, spots, *refs):
    totals = refs[-1]
    totals[...] = jnp.zeros_like(totals)
    for (group, flag), stack in zip(groups, refs):
        base = far + 2 + group * slots
        found = lists[group]
        if flag is not None:
            found = jnp.where(lists[far + 1] == flag, found, 0)
        add_pairs(owned, found, base, lists, stack, spots, totals)


def first_kernel(owned, far, slots, lists, coords, stack, totals, spots):
    totals[...] = jnp.zeros_like(totals)
    turned = 4.0 * jnp.transpose(coords[...])
    for tile in range(owned):
        spread_tile(spots, tile, turned, tile, 2 * owned)
    add_pairs(owned, lists[0], far + 2, lists, stack, spots, totals)


def far_kernel(rows, owned, far, slots, lists, *refs):
    points = refs[:2]
    stacks = refs[2 : 2 + far]
    outs = refs[2 + far : 1 + far + rows]
    slab, spots, totals, wanted = refs[1 + far + rows :]
    stride = 2 * owned
    spread = 3 * stride
    found = lists[far]
    base = far + 2 + far * slots

    @pl.when(found == 0)
    def _():
        for out in outs:
            out[...] = jnp.zeros_like(out)

    @pl.when(found > 0)
    def _():
        for tile in range((rows - 1) * owned):
            wanted[tile] = 0

        def want(slot, carry):
            wanted[lists[base + slot] & 255] = 1
            return carry

        lax.fori_loop(0, found, want, jnp.int32(0))
        totals[...] = jnp.zeros_like(totals)
        top = 0
        for stack in stacks:
            slab[pl.ds(top, stack.shape[0]), :] = stack[...]
            top += stack.shape[0]
        for place, mask in enumerate(masks(rows)):
            if mask:
                top = (place % (rows // 2)) * spread
                turned = 4.0 * jnp.transpose(points[place // (rows // 2)][pl.ds(top, spread), :])
                for tile in range(owned):
                    slot = (mask - 1) * owned + tile

                    @pl.when(wanted[slot] == 1)
                    def _():
                        spread_tile(spots, slot, turned, tile, stride)

        add_pairs(owned, found, base, lists, slab, spots, totals)
        for at in range(rows - 1):
            outs[at][...] = totals[pl.ds(at * stride, stride)]


def sums_kernel(terms, residual_ref, direction_ref, noise_ref, *refs):
    partials = refs[:terms]
    applied_ref, stats_ref, stack = refs[terms:]
    halves = noise_ref.shape[0]
    zero = jnp.zeros((SIDES, LANES), jnp.float32)
    now, bend, cross, size = zero, zero, zero, zero
    for part in range(halves):
        total = partials[0][part]
        for other in partials[1:]:
            total = total + other[part]
        residual = residual_ref[pl.ds(part, SIDES, stride=halves), :]
        direction = direction_ref[pl.ds(part, SIDES, stride=halves), :]
        applied = noise_ref[part : part + 1, :] * direction + SCALED_KERNEL * total
        applied_ref[part] = applied
        now = now + residual * residual
        bend = bend + direction * applied
        cross = cross + residual * applied
        size = size + applied * applied
    stack[...] = jnp.zeros_like(stack)
    for slot, value in enumerate((now, bend, cross, size)):
        stack[SIDES * slot : SIDES * slot + SIDES, :] = value
    stats_ref[...] = lax.dot_general(
        jnp.ones((stats_ref.shape[0], LANES), jnp.float32),
        stack[...],
        (((1,), (1,)), ((), ())),
        precision=lax.Precision.HIGHEST,
        preferred_element_type=jnp.float32,
    )


def step_kernel(
    stats_ref, applied_ref, solution_ref, residual_ref, direction_ref, new_x, new_r, new_d
):
    halves = applied_ref.shape[0]
    summed = jnp.sum(stats_ref[...], axis=0, keepdims=True)
    summed = jnp.broadcast_to(summed, (SIDES, LANES))
    lane = lax.broadcasted_iota(jnp.int32, (SIDES, LANES), 1)
    line = lax.broadcasted_iota(jnp.int32, (SIDES, LANES), 0)

    def pick(slot):
        return jnp.sum(
            jnp.where(lane == line + SIDES * slot, summed, 0.0), axis=1, keepdims=True
        )

    now, bend, cross, size = pick(0), pick(1), pick(2), pick(3)
    step = now / bend
    after = jnp.maximum(now - 2.0 * step * cross + step * step * size, 0.0)
    beta = jnp.broadcast_to(after / (now + EPS), (SIDES, LANES))
    step = jnp.broadcast_to(step, (SIDES, LANES))
    for part in range(halves):
        place = pl.ds(part, SIDES, stride=halves)
        direction = direction_ref[place, :]
        new_x[place, :] = solution_ref[place, :] + step * direction
        residual = residual_ref[place, :] - step * applied_ref[part]
        new_r[place, :] = residual
        new_d[place, :] = residual + beta * direction


def per_device(rows, cols, solution, residual, direction, noise_var, coords, tile_pairs, tile_count):
    sides, owned, _, _, tile_size = direction.shape
    assert sides == SIDES and tile_size == 2 * LANES
    assert tile_pairs.shape[-1] % 4 == 0 and (rows - 1) * owned <= 256
    assert rows & (rows - 1) == 0 and cols & (cols - 1) == 0 and cols >= rows > 1 and cols > 2
    parts = rows * cols
    halves = 2 * owned
    flat_x = solution.reshape(-1, LANES)
    flat_r = residual.reshape(-1, LANES)
    flat_d = direction.reshape(-1, LANES)
    flat_c = coords.reshape(-1, LANES)
    pairs = tile_pairs.reshape(2, -1)
    slots = pairs.shape[1]
    vmem = pl.BlockSpec(memory_space=pltpu.VMEM)
    smem = pl.BlockSpec(memory_space=pltpu.SMEM)
    hbm = pl.BlockSpec(memory_space=pltpu.HBM)
    block = jax.ShapeDtypeStruct((halves, sides, LANES), jnp.float32)
    flat = jax.ShapeDtypeStruct(flat_d.shape, jnp.float32)

    def hop(value, axis, size, bit):
        return lax.ppermute(value, axis, [(at, at ^ bit) for at in range(size)])

    bits_s, bits_c = bits_of(cols)[:-1], bits_of(rows)
    stages = len(bits_s)
    assert stages > 1 and stages >= len(bits_c) - 1
    far = 2 * stages
    lists = pl.pallas_call(
        functools.partial(plan_kernel, rows, cols, owned),
        out_shape=jax.ShapeDtypeStruct((far + 2 + (far + 1) * slots,), jnp.int32),
        in_specs=[smem, hbm],
        out_specs=smem,
        scratch_shapes=[
            pltpu.SMEM(pairs.shape, jnp.int32),
            pltpu.SMEM((far + 1,), jnp.int32),
            pltpu.SemaphoreType.DMA(()),
        ],
        compiler_params=pltpu.CompilerParams(vmem_limit_bytes=8 << 20),
        cost_estimate=pl.CostEstimate(flops=10**9, bytes_accessed=10**5, transcendentals=0),
        name="plan",
    )(tile_count, pltpu.with_memory_space_constraint(pairs, pltpu.HBM))

    def near(groups, stacks):
        return pl.pallas_call(
            functools.partial(near_kernel, owned, groups, far, slots),
            out_shape=block,
            in_specs=[smem] + [vmem] * (1 + len(stacks)),
            out_specs=vmem,
            compiler_params=pltpu.CompilerParams(vmem_limit_bytes=16 << 20),
            cost_estimate=pl.CostEstimate(flops=10**10, bytes_accessed=10**6, transcendentals=0),
            name="near",
        )(lists, spots, *stacks)

    moved = [hop(flat_d, "col", cols, bits_s[0]), hop(flat_c, "col", cols, bits_s[0])]
    held_c = flat_c
    moved_c = hop(held_c, "row", rows, bits_c[0])
    *moved, moved_c, lists = lax.optimization_barrier((*moved, moved_c, lists))
    stacks = [lax.optimization_barrier(jnp.concatenate([flat_d, flat_c] + moved, axis=0))]
    swapped, terms = [], []
    for at in range(stages):
        fresh = None
        if at < stages - 1:
            sent = stacks[0] if at == 0 else jnp.concatenate(stacks, axis=0)
            fresh = hop(sent, "col", cols, bits_s[at + 1])
        swapped.append(hop(stacks[at], "col", cols, 1))
        if at == 0:
            term, spots = pl.pallas_call(
                functools.partial(first_kernel, owned, far, slots),
                out_shape=[
                    block,
                    jax.ShapeDtypeStruct((owned, 3, tile_size, LANES), jnp.float32),
                ],
                in_specs=[smem, vmem, vmem],
                out_specs=[vmem] * 2,
                compiler_params=pltpu.CompilerParams(vmem_limit_bytes=16 << 20),
                cost_estimate=pl.CostEstimate(
                    flops=10**10, bytes_accessed=10**6, transcendentals=0
                ),
                name="first",
            )(lists, flat_c, stacks[0])
        else:
            term = near([(stages + at - 1, 0)], [swapped[at - 1]])
        term, moved_c, stacks[at] = lax.optimization_barrier((term, moved_c, stacks[at]))
        if at + 1 < len(bits_c):
            held_c = jnp.concatenate([held_c, moved_c], axis=0)
            moved_c = hop(held_c, "row", rows, bits_c[at + 1])
        if fresh is None:
            term, swapped[at] = lax.optimization_barrier((term, swapped[at]))
        else:
            term, fresh = lax.optimization_barrier((term, fresh))
            stacks.append(fresh)
        terms.append(term)
    heights = sum(stack.shape[0] for stack in stacks + swapped)
    partials = pl.pallas_call(
        functools.partial(far_kernel, rows, owned, far, slots),
        out_shape=[block] * (rows - 1),
        in_specs=[smem] + [vmem] * (2 + far),
        out_specs=[vmem] * (rows - 1),
        scratch_shapes=[
            pltpu.VMEM((heights, LANES), jnp.float32),
            pltpu.VMEM(((rows - 1) * owned, 3, tile_size, LANES), jnp.float32),
            pltpu.VMEM(((rows - 1) * halves, sides, LANES), jnp.float32),
            pltpu.SMEM(((rows - 1) * owned,), jnp.int32),
        ],
        compiler_params=pltpu.CompilerParams(vmem_limit_bytes=36 << 20),
        cost_estimate=pl.CostEstimate(flops=10**10, bytes_accessed=10**6, transcendentals=0),
        name="far",
    )(lists, held_c, moved_c, *stacks, *swapped)
    *partials, spots = lax.optimization_barrier((*partials, spots))
    arrived = [hop(partials[mask - 1], "row", rows, mask) for mask in range(1, rows)]
    late = [(at, None) for at in range(1, stages)] + [(far - 1, None)]
    late = late + [(stages + at, 1) for at in range(stages - 1)]
    terms.append(near(late, stacks[1:] + swapped[-1:] + swapped[:-1]))
    *arrived, terms[-1] = lax.optimization_barrier((*arrived, terms[-1]))
    terms = terms + arrived
    applied, stats = pl.pallas_call(
        functools.partial(sums_kernel, len(terms)),
        out_shape=[block, jax.ShapeDtypeStruct((parts, LANES), jnp.float32)],
        in_specs=[vmem] * (3 + len(terms)),
        out_specs=[vmem] * 2,
        scratch_shapes=[pltpu.VMEM((LANES, LANES), jnp.float32)],
        compiler_params=pltpu.CompilerParams(vmem_limit_bytes=4 << 20),
        name="sums",
    )(flat_r, flat_d, noise_var.reshape(-1, LANES), *terms)
    stats = lax.all_to_all(stats, ("row", "col"), 0, 0, tiled=True)
    new_x, new_r, new_d = pl.pallas_call(
        step_kernel,
        out_shape=[flat] * 3,
        in_specs=[vmem] * 5,
        out_specs=[vmem] * 3,
        compiler_params=pltpu.CompilerParams(vmem_limit_bytes=4 << 20),
        name="step",
    )(stats, applied, flat_x, flat_r, flat_d)
    return tuple(new.reshape(direction.shape) for new in (new_x, new_r, new_d))


def solution(mesh):
    field = P(None, None, "row", "col", None)
    in_specs = (
        field,
        field,
        field,
        P(None, "row", "col", None),
        field,
        P(None, "row", "col", None),
        P("row", "col"),
    )
    return jax.shard_map(
        functools.partial(per_device, mesh.shape["row"], mesh.shape["col"]),
        mesh=mesh,
        in_specs=in_specs,
        out_specs=(field, field, field),
        check_vma=False,
    )
```

```python
import functools
import jax
import jax.numpy as jnp
from jax import lax
from jax.experimental import pallas as pl
from jax.experimental.pallas import tpu as pltpu
from jax.sharding import PartitionSpec as P

EPS = 1e-06
SCALED_KERNEL = 0.125 / 256.0
TINY = 1e-30
LANES = 128
SIDES = 8
GROUP = 8


def bits_of(size):
    found = []
    bit = size // 2
    while bit:
        found.append(bit)
        bit //= 2
    return found


def spread_tile(spots, slot, turned, tile, stride):
    for axis in range(3):
        for half in range(2):
            lane = axis * stride + 2 * tile + half
            spots[slot, axis, pl.ds(LANES * half, LANES), :] = jnp.broadcast_to(
                turned[:, lane : lane + 1], (LANES, LANES)
            )


def plan_kernel(rows, cols, owned, count, pairs_hbm, lists, pairs, tally, sem):
    copy = pltpu.make_async_copy(pairs_hbm, pairs, sem)
    copy.start()
    my_row = lax.axis_index("row")
    my_col = lax.axis_index("col")
    bits = bits_of(cols)[:-1]
    stages = len(bits)
    far = 2 * stages
    height = (SIDES + 3) * 2 * owned
    slots = pairs.shape[1]
    head = far + 2
    for at in range(far + 1):
        tally[at] = 0
    live = count[0, 0]
    copy.wait()

    def sort_four(step, carry):
        sorted_pairs = []
        for part in range(4):
            slot = 4 * step + part
            row_tile = pairs[0, slot]
            col_tile = pairs[1, slot]
            source = lax.bitwise_xor(row_tile & (cols - 1), my_col)
            target = lax.bitwise_xor(col_tile & (rows - 1), my_row)
            core = source & 1
            goal = lax.shift_right_logical(col_tile, rows.bit_length() - 1)
            place = lax.shift_right_logical(source, bits[0].bit_length() - 1) & 1
            near_place = place
            group = core * stages
            for at in range(1, stages):
                here = lax.shift_right_logical(source, bits[at].bit_length() - 1) & 1
                group = jnp.where(here == 1, at + core * stages, group)
                near_place = jnp.where(here == 1, place, near_place)
                place = place + here * 2**at
            is_near = target == 0
            group = jnp.where(is_near, group, far)
            place = jnp.where(is_near, near_place, place + core * (cols // 2))
            goal = jnp.where(is_near, goal, goal + (target - 1) * owned)
            top = place * height + 2 * lax.shift_right_logical(row_tile, cols.bit_length() - 1)
            sorted_pairs.append((group, top * 256 + goal, (slot < live).astype(jnp.int32)))
        for group, entry, kept in sorted_pairs:
            found = tally[group]
            lists[head + group * slots + found] = entry
            tally[group] = found + kept
        return carry

    lax.fori_loop(0, lax.shift_right_logical(live + 3, 2), sort_four, jnp.int32(0))
    for at in range(far + 1):
        lists[at] = tally[at]
    lists[far + 1] = (4 * tally[far] > tally[stages]).astype(jnp.int32)


def add_pairs(owned, found, base, lists, stack, spots, totals):
    stride = 2 * owned
    held = SIDES * stride

    def add_pair(slot):
        entry = lists[base + slot]
        top = lax.shift_right_logical(entry, 8)
        goal = entry & 255
        lhs_parts, near = [], []
        for side in range(2):
            values = stack[pl.ds(top + side, SIDES, stride=stride), :]
            lead = values.astype(jnp.bfloat16)
            rest = (values - lead.astype(jnp.float32)).astype(jnp.bfloat16)
            lhs_parts.append(jnp.concatenate([lead, rest], axis=0))
            near.append(
                [
                    jnp.broadcast_to(4.0 * stack[pl.ds(top + held + axis * stride + side, 1), :], (16, LANES))
                    for axis in range(3)
                ]
            )
        high_parts, low_parts = [], []
        for step in range(2 * LANES // 16):
            grid = [spots[goal, axis, pl.ds(16 * step, 16), :] for axis in range(3)]
            halves_high, halves_low = [], []
            for side in range(2):
                dx = grid[0] - near[side][0]
                dy = grid[1] - near[side][1]
                dz = grid[2] - near[side][2]
                square = dx * dx + dy * dy + dz * dz
                distance = square * lax.rsqrt(jnp.maximum(square, TINY))
                left = jnp.maximum(4.0 - distance, 0.0)
                left = left * left
                weight = left * left * (distance + 1.0)
                high = weight.astype(jnp.bfloat16)
                halves_high.append(high)
                halves_low.append((weight - high.astype(jnp.float32)).astype(jnp.bfloat16))
            high_parts.append(jnp.concatenate(halves_high, axis=1))
            low_parts.append(jnp.concatenate(halves_low, axis=1))
        lhs = jnp.concatenate(lhs_parts, axis=1)
        dims = (((1,), (1,)), ((), ()))
        product = lax.dot_general(
            lhs, jnp.concatenate(high_parts, axis=0), dims, preferred_element_type=jnp.float32
        ) + lax.dot_general(
            lhs, jnp.concatenate(low_parts, axis=0), dims, preferred_element_type=jnp.float32
        )
        summed = product[:SIDES] + product[SIDES:]
        for half in range(2):
            totals[2 * goal + half] += summed[:, LANES * half : LANES * half + LANES]

    whole = lax.div(found, GROUP)

    def add_group(step, carry):
        for part in range(GROUP):
            add_pair(GROUP * step + part)
        return carry

    def add_one(slot, carry):
        add_pair(slot)
        return carry

    lax.fori_loop(0, whole, add_group, jnp.int32(0))
    lax.fori_loop(GROUP * whole, found, add_one, jnp.int32(0))


def near_kernel(owned, groups, far, slots, lists, spots, *refs):
    totals = refs[-1]
    totals[...] = jnp.zeros_like(totals)
    for (group, flag), stack in zip(groups, refs):
        base = far + 2 + group * slots
        found = lists[group]
        if flag is not None:
            found = jnp.where(lists[far + 1] == flag, found, 0)
        add_pairs(owned, found, base, lists, stack, spots, totals)


def first_kernel(owned, far, slots, lists, coords, stack, totals, spots):
    totals[...] = jnp.zeros_like(totals)
    turned = 4.0 * jnp.transpose(coords[...])
    for tile in range(owned):
        spread_tile(spots, tile, turned, tile, 2 * owned)
    add_pairs(owned, lists[0], far + 2, lists, stack, spots, totals)


def far_kernel(rows, owned, far, slots, lists, *refs):
    points = refs[: rows - 1]
    stacks = refs[rows - 1 : rows - 1 + far]
    outs = refs[rows - 1 + far : 2 * rows - 2 + far]
    slab, spots, totals, wanted = refs[2 * rows - 2 + far :]
    stride = 2 * owned
    found = lists[far]
    base = far + 2 + far * slots

    @pl.when(found == 0)
    def _():
        for out in outs:
            out[...] = jnp.zeros_like(out)

    @pl.when(found > 0)
    def _():
        for tile in range((rows - 1) * owned):
            wanted[tile] = 0

        def want(slot, carry):
            wanted[lists[base + slot] & 255] = 1
            return carry

        lax.fori_loop(0, found, want, jnp.int32(0))
        totals[...] = jnp.zeros_like(totals)
        top = 0
        for stack in stacks:
            slab[pl.ds(top, stack.shape[0]), :] = stack[...]
            top += stack.shape[0]
        for at, part in enumerate(points):
            turned = 4.0 * jnp.transpose(part[...])
            for tile in range(owned):
                slot = at * owned + tile

                @pl.when(wanted[slot] == 1)
                def _():
                    spread_tile(spots, slot, turned, tile, stride)

        add_pairs(owned, found, base, lists, slab, spots, totals)
        for at in range(rows - 1):
            outs[at][...] = totals[pl.ds(at * stride, stride)]


def sums_kernel(terms, residual_ref, direction_ref, noise_ref, *refs):
    partials = refs[:terms]
    applied_ref, stats_ref, stack = refs[terms:]
    halves = noise_ref.shape[0]
    zero = jnp.zeros((SIDES, LANES), jnp.float32)
    now, bend, cross, size = zero, zero, zero, zero
    for part in range(halves):
        total = partials[0][part]
        for other in partials[1:]:
            total = total + other[part]
        residual = residual_ref[pl.ds(part, SIDES, stride=halves), :]
        direction = direction_ref[pl.ds(part, SIDES, stride=halves), :]
        applied = noise_ref[part : part + 1, :] * direction + SCALED_KERNEL * total
        applied_ref[part] = applied
        now = now + residual * residual
        bend = bend + direction * applied
        cross = cross + residual * applied
        size = size + applied * applied
    stack[...] = jnp.zeros_like(stack)
    for slot, value in enumerate((now, bend, cross, size)):
        stack[SIDES * slot : SIDES * slot + SIDES, :] = value
    stats_ref[...] = lax.dot_general(
        jnp.ones((stats_ref.shape[0], LANES), jnp.float32),
        stack[...],
        (((1,), (1,)), ((), ())),
        precision=lax.Precision.HIGHEST,
        preferred_element_type=jnp.float32,
    )


def step_kernel(
    stats_ref, applied_ref, solution_ref, residual_ref, direction_ref, new_x, new_r, new_d
):
    halves = applied_ref.shape[0]
    summed = jnp.sum(stats_ref[...], axis=0, keepdims=True)
    summed = jnp.broadcast_to(summed, (SIDES, LANES))
    lane = lax.broadcasted_iota(jnp.int32, (SIDES, LANES), 1)
    line = lax.broadcasted_iota(jnp.int32, (SIDES, LANES), 0)

    def pick(slot):
        return jnp.sum(
            jnp.where(lane == line + SIDES * slot, summed, 0.0), axis=1, keepdims=True
        )

    now, bend, cross, size = pick(0), pick(1), pick(2), pick(3)
    step = now / bend
    after = jnp.maximum(now - 2.0 * step * cross + step * step * size, 0.0)
    beta = jnp.broadcast_to(after / (now + EPS), (SIDES, LANES))
    step = jnp.broadcast_to(step, (SIDES, LANES))
    for part in range(halves):
        place = pl.ds(part, SIDES, stride=halves)
        direction = direction_ref[place, :]
        new_x[place, :] = solution_ref[place, :] + step * direction
        residual = residual_ref[place, :] - step * applied_ref[part]
        new_r[place, :] = residual
        new_d[place, :] = residual + beta * direction


def per_device(rows, cols, solution, residual, direction, noise_var, coords, tile_pairs, tile_count):
    sides, owned, _, _, tile_size = direction.shape
    assert sides == SIDES and tile_size == 2 * LANES
    assert tile_pairs.shape[-1] % 4 == 0 and (rows - 1) * owned <= 256
    assert rows & (rows - 1) == 0 and cols & (cols - 1) == 0 and cols >= rows > 1 and cols > 2
    parts = rows * cols
    halves = 2 * owned
    flat_x = solution.reshape(-1, LANES)
    flat_r = residual.reshape(-1, LANES)
    flat_d = direction.reshape(-1, LANES)
    flat_c = coords.reshape(-1, LANES)
    pairs = tile_pairs.reshape(2, -1)
    slots = pairs.shape[1]
    vmem = pl.BlockSpec(memory_space=pltpu.VMEM)
    smem = pl.BlockSpec(memory_space=pltpu.SMEM)
    hbm = pl.BlockSpec(memory_space=pltpu.HBM)
    block = jax.ShapeDtypeStruct((halves, sides, LANES), jnp.float32)
    flat = jax.ShapeDtypeStruct(flat_d.shape, jnp.float32)

    def hop(value, axis, size, bit):
        return lax.ppermute(value, axis, [(at, at ^ bit) for at in range(size)])

    bits_s = bits_of(cols)[:-1]
    stages = len(bits_s)
    assert stages > 1
    far = 2 * stages
    lists = pl.pallas_call(
        functools.partial(plan_kernel, rows, cols, owned),
        out_shape=jax.ShapeDtypeStruct((far + 2 + (far + 1) * slots,), jnp.int32),
        in_specs=[smem, hbm],
        out_specs=smem,
        scratch_shapes=[
            pltpu.SMEM(pairs.shape, jnp.int32),
            pltpu.SMEM((far + 1,), jnp.int32),
            pltpu.SemaphoreType.DMA(()),
        ],
        compiler_params=pltpu.CompilerParams(vmem_limit_bytes=8 << 20),
        cost_estimate=pl.CostEstimate(flops=10**9, bytes_accessed=10**5, transcendentals=0),
        name="plan",
    )(tile_count, pltpu.with_memory_space_constraint(pairs, pltpu.HBM))

    def near(groups, stacks):
        return pl.pallas_call(
            functools.partial(near_kernel, owned, groups, far, slots),
            out_shape=block,
            in_specs=[smem] + [vmem] * (1 + len(stacks)),
            out_specs=vmem,
            compiler_params=pltpu.CompilerParams(vmem_limit_bytes=16 << 20),
            cost_estimate=pl.CostEstimate(flops=10**10, bytes_accessed=10**6, transcendentals=0),
            name="near",
        )(lists, spots, *stacks)

    moved = [hop(flat_d, "col", cols, bits_s[0]), hop(flat_c, "col", cols, bits_s[0])]
    around = [hop(flat_c, "row", rows, mask) for mask in range(1, rows)]
    *moved, lists = lax.optimization_barrier((*moved, *around, lists))
    moved, around = moved[:2], moved[2:]
    stacks = [lax.optimization_barrier(jnp.concatenate([flat_d, flat_c] + moved, axis=0))]
    swapped, terms = [], []
    for at in range(stages):
        fresh = None
        if at < stages - 1:
            sent = stacks[0] if at == 0 else jnp.concatenate(stacks, axis=0)
            fresh = hop(sent, "col", cols, bits_s[at + 1])
        swapped.append(hop(stacks[at], "col", cols, 1))
        if at == 0:
            term, spots = pl.pallas_call(
                functools.partial(first_kernel, owned, far, slots),
                out_shape=[
                    block,
                    jax.ShapeDtypeStruct((owned, 3, tile_size, LANES), jnp.float32),
                ],
                in_specs=[smem, vmem, vmem],
                out_specs=[vmem] * 2,
                compiler_params=pltpu.CompilerParams(vmem_limit_bytes=16 << 20),
                cost_estimate=pl.CostEstimate(
                    flops=10**10, bytes_accessed=10**6, transcendentals=0
                ),
                name="first",
            )(lists, flat_c, stacks[0])
        else:
            term = near([(stages + at - 1, 0)], [swapped[at - 1]])
        if fresh is None:
            term, swapped[at] = lax.optimization_barrier((term, swapped[at]))
        else:
            term, fresh = lax.optimization_barrier((term, fresh))
            stacks.append(fresh)
        terms.append(term)
    heights = sum(stack.shape[0] for stack in stacks + swapped)
    partials = pl.pallas_call(
        functools.partial(far_kernel, rows, owned, far, slots),
        out_shape=[block] * (rows - 1),
        in_specs=[smem] + [vmem] * (rows - 1 + far),
        out_specs=[vmem] * (rows - 1),
        scratch_shapes=[
            pltpu.VMEM((heights, LANES), jnp.float32),
            pltpu.VMEM(((rows - 1) * owned, 3, tile_size, LANES), jnp.float32),
            pltpu.VMEM(((rows - 1) * halves, sides, LANES), jnp.float32),
            pltpu.SMEM(((rows - 1) * owned,), jnp.int32),
        ],
        compiler_params=pltpu.CompilerParams(vmem_limit_bytes=36 << 20),
        cost_estimate=pl.CostEstimate(flops=10**10, bytes_accessed=10**6, transcendentals=0),
        name="far",
    )(lists, *around, *stacks, *swapped)
    *partials, spots = lax.optimization_barrier((*partials, spots))
    arrived = [hop(partials[mask - 1], "row", rows, mask) for mask in range(1, rows)]
    late = [(at, None) for at in range(1, stages)] + [(far - 1, None)]
    late = late + [(stages + at, 1) for at in range(stages - 1)]
    terms.append(near(late, stacks[1:] + swapped[-1:] + swapped[:-1]))
    *arrived, terms[-1] = lax.optimization_barrier((*arrived, terms[-1]))
    terms = terms + arrived
    applied, stats = pl.pallas_call(
        functools.partial(sums_kernel, len(terms)),
        out_shape=[block, jax.ShapeDtypeStruct((parts, LANES), jnp.float32)],
        in_specs=[vmem] * (3 + len(terms)),
        out_specs=[vmem] * 2,
        scratch_shapes=[pltpu.VMEM((LANES, LANES), jnp.float32)],
        compiler_params=pltpu.CompilerParams(vmem_limit_bytes=4 << 20),
        name="sums",
    )(flat_r, flat_d, noise_var.reshape(-1, LANES), *terms)
    stats = lax.all_to_all(stats, ("row", "col"), 0, 0, tiled=True)
    new_x, new_r, new_d = pl.pallas_call(
        step_kernel,
        out_shape=[flat] * 3,
        in_specs=[vmem] * 5,
        out_specs=[vmem] * 3,
        compiler_params=pltpu.CompilerParams(vmem_limit_bytes=4 << 20),
        name="step",
    )(stats, applied, flat_x, flat_r, flat_d)
    return tuple(new.reshape(direction.shape) for new in (new_x, new_r, new_d))


def solution(mesh):
    field = P(None, None, "row", "col", None)
    in_specs = (
        field,
        field,
        field,
        P(None, "row", "col", None),
        field,
        P(None, "row", "col", None),
        P("row", "col"),
    )
    return jax.shard_map(
        functools.partial(per_device, mesh.shape["row"], mesh.shape["col"]),
        mesh=mesh,
        in_specs=in_specs,
        out_specs=(field, field, field),
        check_vma=False,
    )
```

```python
import functools
import jax
import jax.numpy as jnp
from jax import lax
from jax.experimental import pallas as pl
from jax.experimental.pallas import tpu as pltpu
from jax.sharding import PartitionSpec as P

EPS = 1e-06
SCALED_KERNEL = 0.125 / 256.0
TINY = 1e-30
LANES = 128
SIDES = 8
GROUP = 8


def bits_of(size):
    found = []
    bit = size // 2
    while bit:
        found.append(bit)
        bit //= 2
    return found


def masks(size):
    found = [0]
    for bit in bits_of(size):
        found = found + [mask ^ bit for mask in found]
    return found


def spread_tile(spots, slot, turned, tile, stride):
    for axis in range(3):
        for half in range(2):
            lane = axis * stride + 2 * tile + half
            spots[slot, axis, pl.ds(LANES * half, LANES), :] = jnp.broadcast_to(
                turned[:, lane : lane + 1], (LANES, LANES)
            )


def plan_kernel(rows, cols, owned, count, pairs_hbm, lists, pairs, tally, sem):
    copy = pltpu.make_async_copy(pairs_hbm, pairs, sem)
    copy.start()
    my_row = lax.axis_index("row")
    my_col = lax.axis_index("col")
    bits = bits_of(cols)[:-1]
    stages = len(bits)
    far = 2 * stages
    height = (SIDES + 3) * 2 * owned
    slots = pairs.shape[1]
    head = far + 2
    for at in range(far + 1):
        tally[at] = 0
    live = count[0, 0]
    copy.wait()

    def sort_four(step, carry):
        sorted_pairs = []
        for part in range(4):
            slot = 4 * step + part
            row_tile = pairs[0, slot]
            col_tile = pairs[1, slot]
            source = lax.bitwise_xor(row_tile & (cols - 1), my_col)
            target = lax.bitwise_xor(col_tile & (rows - 1), my_row)
            core = source & 1
            goal = lax.shift_right_logical(col_tile, rows.bit_length() - 1)
            place = lax.shift_right_logical(source, bits[0].bit_length() - 1) & 1
            near_place = place
            group = core * stages
            for at in range(1, stages):
                here = lax.shift_right_logical(source, bits[at].bit_length() - 1) & 1
                group = jnp.where(here == 1, at + core * stages, group)
                near_place = jnp.where(here == 1, place, near_place)
                place = place + here * 2**at
            is_near = target == 0
            group = jnp.where(is_near, group, far)
            place = jnp.where(is_near, near_place, place + core * (cols // 2))
            goal = jnp.where(is_near, goal, goal + (target - 1) * owned)
            top = place * height + 2 * lax.shift_right_logical(row_tile, cols.bit_length() - 1)
            sorted_pairs.append((group, top * 256 + goal, (slot < live).astype(jnp.int32)))
        for group, entry, kept in sorted_pairs:
            found = tally[group]
            lists[head + group * slots + found] = entry
            tally[group] = found + kept
        return carry

    lax.fori_loop(0, lax.shift_right_logical(live + 3, 2), sort_four, jnp.int32(0))
    for at in range(far + 1):
        lists[at] = tally[at]
    lists[far + 1] = (4 * tally[far] > tally[stages]).astype(jnp.int32)


def add_pairs(owned, found, base, lists, stack, spots, totals):
    stride = 2 * owned
    held = SIDES * stride

    def add_pair(slot):
        entry = lists[base + slot]
        top = lax.shift_right_logical(entry, 8)
        goal = entry & 255
        lhs_parts, near = [], []
        for side in range(2):
            values = stack[pl.ds(top + side, SIDES, stride=stride), :]
            lead = values.astype(jnp.bfloat16)
            rest = (values - lead.astype(jnp.float32)).astype(jnp.bfloat16)
            lhs_parts.append(jnp.concatenate([lead, rest], axis=0))
            near.append(
                [
                    jnp.broadcast_to(4.0 * stack[pl.ds(top + held + axis * stride + side, 1), :], (16, LANES))
                    for axis in range(3)
                ]
            )
        high_parts, low_parts = [], []
        for step in range(2 * LANES // 16):
            grid = [spots[goal, axis, pl.ds(16 * step, 16), :] for axis in range(3)]
            halves_high, halves_low = [], []
            for side in range(2):
                dx = grid[0] - near[side][0]
                dy = grid[1] - near[side][1]
                dz = grid[2] - near[side][2]
                square = dx * dx + dy * dy + dz * dz
                distance = square * lax.rsqrt(jnp.maximum(square, TINY))
                left = jnp.maximum(4.0 - distance, 0.0)
                left = left * left
                weight = left * left * (distance + 1.0)
                high = weight.astype(jnp.bfloat16)
                halves_high.append(high)
                halves_low.append((weight - high.astype(jnp.float32)).astype(jnp.bfloat16))
            high_parts.append(jnp.concatenate(halves_high, axis=1))
            low_parts.append(jnp.concatenate(halves_low, axis=1))
        lhs = jnp.concatenate(lhs_parts, axis=1)
        dims = (((1,), (1,)), ((), ()))
        product = lax.dot_general(
            lhs, jnp.concatenate(high_parts, axis=0), dims, preferred_element_type=jnp.float32
        ) + lax.dot_general(
            lhs, jnp.concatenate(low_parts, axis=0), dims, preferred_element_type=jnp.float32
        )
        summed = product[:SIDES] + product[SIDES:]
        for half in range(2):
            totals[2 * goal + half] += summed[:, LANES * half : LANES * half + LANES]

    whole = lax.div(found, GROUP)

    def add_group(step, carry):
        for part in range(GROUP):
            add_pair(GROUP * step + part)
        return carry

    def add_one(slot, carry):
        add_pair(slot)
        return carry

    lax.fori_loop(0, whole, add_group, jnp.int32(0))
    half = GROUP // 2
    more = found - GROUP * whole >= half

    @pl.when(more)
    def _():
        for part in range(half):
            add_pair(GROUP * whole + part)

    lax.fori_loop(GROUP * whole + jnp.where(more, half, 0), found, add_one, jnp.int32(0))


def near_kernel(owned, groups, far, slots, lists, spots, *refs):
    totals = refs[-1]
    totals[...] = jnp.zeros_like(totals)
    for (group, flag), stack in zip(groups, refs):
        base = far + 2 + group * slots
        found = lists[group]
        if flag is not None:
            found = jnp.where(lists[far + 1] == flag, found, 0)
        add_pairs(owned, found, base, lists, stack, spots, totals)


def first_kernel(owned, far, slots, lists, coords, stack, totals, spots):
    totals[...] = jnp.zeros_like(totals)
    turned = 4.0 * jnp.transpose(coords[...])
    for tile in range(owned):
        spread_tile(spots, tile, turned, tile, 2 * owned)
    add_pairs(owned, lists[0], far + 2, lists, stack, spots, totals)


def far_kernel(rows, owned, far, slots, lists, *refs):
    points = refs[:2]
    stacks = refs[2 : 2 + far]
    outs = refs[2 + far : 1 + far + rows]
    slab, spots, totals, wanted = refs[1 + far + rows :]
    stride = 2 * owned
    spread = 3 * stride
    found = lists[far]
    base = far + 2 + far * slots

    @pl.when(found == 0)
    def _():
        for out in outs:
            out[...] = jnp.zeros_like(out)

    @pl.when(found > 0)
    def _():
        for tile in range((rows - 1) * owned):
            wanted[tile] = 0

        def want(slot, carry):
            wanted[lists[base + slot] & 255] = 1
            return carry

        lax.fori_loop(0, found, want, jnp.int32(0))
        totals[...] = jnp.zeros_like(totals)
        top = 0
        for stack in stacks:
            slab[pl.ds(top, stack.shape[0]), :] = stack[...]
            top += stack.shape[0]
        for place, mask in enumerate(masks(rows)):
            if mask:
                top = (place % (rows // 2)) * spread
                turned = 4.0 * jnp.transpose(points[place // (rows // 2)][pl.ds(top, spread), :])
                for tile in range(owned):
                    slot = (mask - 1) * owned + tile

                    @pl.when(wanted[slot] == 1)
                    def _():
                        spread_tile(spots, slot, turned, tile, stride)

        add_pairs(owned, found, base, lists, slab, spots, totals)
        for at in range(rows - 1):
            outs[at][...] = totals[pl.ds(at * stride, stride)]


def sums_kernel(terms, residual_ref, direction_ref, noise_ref, *refs):
    partials = refs[:terms]
    applied_ref, stats_ref, stack = refs[terms:]
    halves = noise_ref.shape[0]
    zero = jnp.zeros((SIDES, LANES), jnp.float32)
    now, bend, cross, size = zero, zero, zero, zero
    for part in range(halves):
        total = partials[0][part]
        for other in partials[1:]:
            total = total + other[part]
        residual = residual_ref[pl.ds(part, SIDES, stride=halves), :]
        direction = direction_ref[pl.ds(part, SIDES, stride=halves), :]
        applied = noise_ref[part : part + 1, :] * direction + SCALED_KERNEL * total
        applied_ref[part] = applied
        now = now + residual * residual
        bend = bend + direction * applied
        cross = cross + residual * applied
        size = size + applied * applied
    stack[...] = jnp.zeros_like(stack)
    for slot, value in enumerate((now, bend, cross, size)):
        stack[SIDES * slot : SIDES * slot + SIDES, :] = value
    stats_ref[...] = lax.dot_general(
        jnp.ones((stats_ref.shape[0], LANES), jnp.float32),
        stack[...],
        (((1,), (1,)), ((), ())),
        precision=lax.Precision.HIGHEST,
        preferred_element_type=jnp.float32,
    )


def step_kernel(
    stats_ref, applied_ref, solution_ref, residual_ref, direction_ref, new_x, new_r, new_d
):
    halves = applied_ref.shape[0]
    summed = jnp.sum(stats_ref[...], axis=0, keepdims=True)
    summed = jnp.broadcast_to(summed, (SIDES, LANES))
    lane = lax.broadcasted_iota(jnp.int32, (SIDES, LANES), 1)
    line = lax.broadcasted_iota(jnp.int32, (SIDES, LANES), 0)

    def pick(slot):
        return jnp.sum(
            jnp.where(lane == line + SIDES * slot, summed, 0.0), axis=1, keepdims=True
        )

    now, bend, cross, size = pick(0), pick(1), pick(2), pick(3)
    step = now / bend
    after = jnp.maximum(now - 2.0 * step * cross + step * step * size, 0.0)
    beta = jnp.broadcast_to(after / (now + EPS), (SIDES, LANES))
    step = jnp.broadcast_to(step, (SIDES, LANES))
    for part in range(halves):
        place = pl.ds(part, SIDES, stride=halves)
        direction = direction_ref[place, :]
        new_x[place, :] = solution_ref[place, :] + step * direction
        residual = residual_ref[place, :] - step * applied_ref[part]
        new_r[place, :] = residual
        new_d[place, :] = residual + beta * direction


def per_device(rows, cols, solution, residual, direction, noise_var, coords, tile_pairs, tile_count):
    sides, owned, _, _, tile_size = direction.shape
    assert sides == SIDES and tile_size == 2 * LANES
    assert tile_pairs.shape[-1] % 4 == 0 and (rows - 1) * owned <= 256
    assert rows & (rows - 1) == 0 and cols & (cols - 1) == 0 and cols >= rows > 1 and cols > 2
    parts = rows * cols
    halves = 2 * owned
    flat_x = solution.reshape(-1, LANES)
    flat_r = residual.reshape(-1, LANES)
    flat_d = direction.reshape(-1, LANES)
    flat_c = coords.reshape(-1, LANES)
    pairs = tile_pairs.reshape(2, -1)
    slots = pairs.shape[1]
    vmem = pl.BlockSpec(memory_space=pltpu.VMEM)
    smem = pl.BlockSpec(memory_space=pltpu.SMEM)
    hbm = pl.BlockSpec(memory_space=pltpu.HBM)
    block = jax.ShapeDtypeStruct((halves, sides, LANES), jnp.float32)
    flat = jax.ShapeDtypeStruct(flat_d.shape, jnp.float32)

    def hop(value, axis, size, bit):
        return lax.ppermute(value, axis, [(at, at ^ bit) for at in range(size)])

    bits_s, bits_c = bits_of(cols)[:-1], bits_of(rows)
    stages = len(bits_s)
    assert stages > 1 and stages >= len(bits_c) - 1
    far = 2 * stages
    lists = pl.pallas_call(
        functools.partial(plan_kernel, rows, cols, owned),
        out_shape=jax.ShapeDtypeStruct((far + 2 + (far + 1) * slots,), jnp.int32),
        in_specs=[smem, hbm],
        out_specs=smem,
        scratch_shapes=[
            pltpu.SMEM(pairs.shape, jnp.int32),
            pltpu.SMEM((far + 1,), jnp.int32),
            pltpu.SemaphoreType.DMA(()),
        ],
        compiler_params=pltpu.CompilerParams(vmem_limit_bytes=8 << 20),
        cost_estimate=pl.CostEstimate(flops=10**9, bytes_accessed=10**5, transcendentals=0),
        name="plan",
    )(tile_count, pltpu.with_memory_space_constraint(pairs, pltpu.HBM))

    def near(groups, stacks):
        return pl.pallas_call(
            functools.partial(near_kernel, owned, groups, far, slots),
            out_shape=block,
            in_specs=[smem] + [vmem] * (1 + len(stacks)),
            out_specs=vmem,
            compiler_params=pltpu.CompilerParams(vmem_limit_bytes=16 << 20),
            cost_estimate=pl.CostEstimate(flops=10**10, bytes_accessed=10**6, transcendentals=0),
            name="near",
        )(lists, spots, *stacks)

    moved = [hop(flat_d, "col", cols, bits_s[0]), hop(flat_c, "col", cols, bits_s[0])]
    held_c = flat_c
    moved_c = hop(held_c, "row", rows, bits_c[0])
    *moved, moved_c, lists = lax.optimization_barrier((*moved, moved_c, lists))
    stacks = [lax.optimization_barrier(jnp.concatenate([flat_d, flat_c] + moved, axis=0))]
    swapped, terms = [], []
    for at in range(stages):
        fresh = None
        if at < stages - 1:
            sent = stacks[0] if at == 0 else jnp.concatenate(stacks, axis=0)
            fresh = hop(sent, "col", cols, bits_s[at + 1])
        if at + 1 < len(bits_c):
            held_c = jnp.concatenate([held_c, moved_c], axis=0)
            moved_c = hop(held_c, "row", rows, bits_c[at + 1])
        swapped.append(hop(stacks[at], "col", cols, 1))
        if at == 0:
            term, spots = pl.pallas_call(
                functools.partial(first_kernel, owned, far, slots),
                out_shape=[
                    block,
                    jax.ShapeDtypeStruct((owned, 3, tile_size, LANES), jnp.float32),
                ],
                in_specs=[smem, vmem, vmem],
                out_specs=[vmem] * 2,
                compiler_params=pltpu.CompilerParams(vmem_limit_bytes=16 << 20),
                cost_estimate=pl.CostEstimate(
                    flops=10**10, bytes_accessed=10**6, transcendentals=0
                ),
                name="first",
            )(lists, flat_c, stacks[0])
        else:
            term = near([(stages + at - 1, 0)], [swapped[at - 1]])
        if fresh is None:
            term, swapped[at], moved_c = lax.optimization_barrier((term, swapped[at], moved_c))
        else:
            term, fresh, moved_c = lax.optimization_barrier((term, fresh, moved_c))
            stacks.append(fresh)
        terms.append(term)
    heights = sum(stack.shape[0] for stack in stacks + swapped)
    partials = pl.pallas_call(
        functools.partial(far_kernel, rows, owned, far, slots),
        out_shape=[block] * (rows - 1),
        in_specs=[smem] + [vmem] * (2 + far),
        out_specs=[vmem] * (rows - 1),
        scratch_shapes=[
            pltpu.VMEM((heights, LANES), jnp.float32),
            pltpu.VMEM(((rows - 1) * owned, 3, tile_size, LANES), jnp.float32),
            pltpu.VMEM(((rows - 1) * halves, sides, LANES), jnp.float32),
            pltpu.SMEM(((rows - 1) * owned,), jnp.int32),
        ],
        compiler_params=pltpu.CompilerParams(vmem_limit_bytes=36 << 20),
        cost_estimate=pl.CostEstimate(flops=10**10, bytes_accessed=10**6, transcendentals=0),
        name="far",
    )(lists, held_c, moved_c, *stacks, *swapped)
    *partials, spots = lax.optimization_barrier((*partials, spots))
    arrived = [hop(partials[mask - 1], "row", rows, mask) for mask in range(1, rows)]
    late = [(at, None) for at in range(1, stages)] + [(far - 1, None)]
    late = late + [(stages + at, 1) for at in range(stages - 1)]
    terms.append(near(late, stacks[1:] + swapped[-1:] + swapped[:-1]))
    *arrived, terms[-1] = lax.optimization_barrier((*arrived, terms[-1]))
    terms = terms + arrived
    applied, stats = pl.pallas_call(
        functools.partial(sums_kernel, len(terms)),
        out_shape=[block, jax.ShapeDtypeStruct((parts, LANES), jnp.float32)],
        in_specs=[vmem] * (3 + len(terms)),
        out_specs=[vmem] * 2,
        scratch_shapes=[pltpu.VMEM((LANES, LANES), jnp.float32)],
        compiler_params=pltpu.CompilerParams(vmem_limit_bytes=4 << 20),
        name="sums",
    )(flat_r, flat_d, noise_var.reshape(-1, LANES), *terms)
    stats = lax.all_to_all(stats, ("row", "col"), 0, 0, tiled=True)
    new_x, new_r, new_d = pl.pallas_call(
        step_kernel,
        out_shape=[flat] * 3,
        in_specs=[vmem] * 5,
        out_specs=[vmem] * 3,
        compiler_params=pltpu.CompilerParams(vmem_limit_bytes=4 << 20),
        name="step",
    )(stats, applied, flat_x, flat_r, flat_d)
    return tuple(new.reshape(direction.shape) for new in (new_x, new_r, new_d))


def solution(mesh):
    field = P(None, None, "row", "col", None)
    in_specs = (
        field,
        field,
        field,
        P(None, "row", "col", None),
        field,
        P(None, "row", "col", None),
        P("row", "col"),
    )
    return jax.shard_map(
        functools.partial(per_device, mesh.shape["row"], mesh.shape["col"]),
        mesh=mesh,
        in_specs=in_specs,
        out_specs=(field, field, field),
        check_vma=False,
    )
```
